256 devices in a mesh: frame: 16 (over y, x), seq: 16 (over z, core).
Axes of the slice: x: 4, y: 4, z: 8, core: 2. Of those that a mesh axis runs over, the one named last changes fastest.
Arguments:
- tokens: bfloat16 [16, 512, 5120], P('frame', 'seq'), may hold values from -6 to 6
- query_rows: bfloat16 [16, 512, 4096], P('frame', 'seq'), may hold values from -40 to 40
- key_rows: bfloat16 [16, 512, 4096], P('frame', 'seq'), may hold values from -40 to 40
- value_rows: bfloat16 [16, 512, 4096], P('frame', 'seq'), may hold values from -6 to 6
- gain_query: float32 [4096], replicated, may hold values from 0.5 to 2.5
- gain_key: float32 [4096], replicated, may hold values from 0.5 to 2.5
- out_weight: bfloat16 [4096, 5120], P('seq'), may hold values from -0.09375 to 0.09375
- out_bias: bfloat16 [5120], replicated, may hold values from -3 to 3
- gate_table: bfloat16 [64, 5120], replicated, may hold values from -12 to 12
- noise_level: int32 [16], replicated, may hold values from 0 to 63
- slot_order: int32 [16], replicated, may hold values from 0 to 1023, as said below
Outputs:
- updated: bfloat16 [16, 512, 5120], P('frame', 'seq')
The draws below stay inside these ranges and needn't reach their ends.
Inputs may be any that keep to these rules, and one draw needn't show every extreme that they name: `slot_order`: all 16 stamps are distinct.
All inputs are finite; a program needn't handle non-finite values.
Results may differ from the reference program's by a relative error of at most 0.013.
Values may be sent and summed in bfloat16 or wider, within the bound.
A program may use at most 64 MiB of HBM per device.

```python
import math
import jax
import jax.numpy as jnp
from jax import lax

D = 5120
HEADS = 32
HD = 128
LEVELS = 64
QK = 4096
FTOK = 512
FRAMES = 16
N_SEQ = 16


def shaped_draw(key, seed_tag):
    drawn = jax.random.normal(jax.random.fold_in(key, seed_tag), (FRAMES, FTOK, QK), jnp.float32)
    return jnp.clip(drawn, -40.0, 40.0)


def draw_query_rows(key, part):
    return shaped_draw(key, 1).astype(jnp.bfloat16)


def draw_key_rows(key, part):
    return shaped_draw(key, 7).astype(jnp.bfloat16)


def draw_slot_order(key, part):
    stamps = jax.random.permutation(jax.random.fold_in(key, 211), 64 * FRAMES)[:FRAMES].astype(jnp.int32)
    highest = jnp.argmax(stamps)
    lowest = jnp.argmin(stamps)
    stamps = stamps.at[highest].set(64 * FRAMES - 1)
    stamps = stamps.at[lowest].set(0)
    return stamps.astype(jnp.int32)


def place_ends(entries, rng, least, high):
    longest = entries.shape.index(max(entries.shape))
    spots = []
    for shift in (0, 1):
        where = [jax.random.randint(jax.random.fold_in(rng, axis), (), 0, length) for axis, length in enumerate(entries.shape)]
        where[longest] = (where[longest] + shift) % entries.shape[longest]
        spots.append(tuple(where))
    return entries.at[spots[0]].set(least).at[spots[1]].set(high)


def block_scale(own_key, extent, cuts, smallest, largest):
    def one(dim, shards_of):
        draws = jax.random.uniform(jax.random.fold_in(jax.random.fold_in(own_key, 6), dim), (shards_of,), jnp.float32, smallest / len(cuts), largest / len(cuts))
        return jnp.repeat(jnp.exp(draws), extent[dim] // shards_of).reshape((-1,) + (1,) * (len(extent) - dim - 1))

    loudness = one(*cuts[0])
    for cut in cuts[1:]:
        loudness = loudness * one(*cut)
    return loudness


def scatter_about(key, dims, scale, reach, cuts=(), dtype=jnp.bfloat16):
    entries = scale * jax.random.normal(key, dims, jnp.float32)
    if cuts:
        entries = entries * block_scale(key, dims, cuts, -0.22, 0.18)
    return jnp.clip(entries, -reach, reach).astype(dtype)


def setup_inputs(seed: int = 0) -> dict:
    key_of = jax.random.split(jax.random.key(seed), 12)
    return {
        "tokens": scatter_about(key_of[0], (FRAMES, FTOK, D), 1.0, 6.0, ((0, 16), (1, 16))),
        "query_rows": draw_query_rows(jax.random.fold_in(key_of[11], 71), 0),
        "key_rows": draw_key_rows(jax.random.fold_in(key_of[11], 71), 0),
        "value_rows": scatter_about(key_of[3], (FRAMES, FTOK, QK), 1.0, 6.0, ((0, 16), (1, 16))),
        "gain_query": jnp.clip(jnp.exp(jax.random.uniform(key_of[4], (QK,), jnp.float32, math.log(0.5), math.log(2.5))), 0.5, 2.5),
        "gain_key": jnp.clip(jnp.exp(jax.random.uniform(key_of[5], (QK,), jnp.float32, math.log(0.5), math.log(2.5))), 0.5, 2.5),
        "out_weight": scatter_about(key_of[6], (QK, D), QK ** -0.5, 0.09375, ((0, 16),)),
        "out_bias": scatter_about(key_of[7], (D,), 0.5, 3.0),
        "gate_table": scatter_about(key_of[8], (LEVELS, D), 3.0, 12.0),
        "noise_level": place_ends(jax.random.randint(key_of[9], (FRAMES,), 0, LEVELS), jax.random.fold_in(key_of[9], 1), 0, LEVELS - 1).astype(jnp.int32),
        "slot_order": draw_slot_order(jax.random.fold_in(key_of[11], 71), 0),
    }


epsilon = 1e-06

def normalize(rows, gain):
    values = rows.astype(jnp.float32)
    inverse = lax.rsqrt(lax.optimization_barrier(jnp.mean(values * values, axis=-1, keepdims=True)) + epsilon)
    return (values * inverse * gain.astype(jnp.float32)).astype(jnp.bfloat16)

def reference(tokens, query_rows, key_rows, value_rows, gain_query, gain_key, out_weight, out_bias, gate_table, noise_level, slot_order):
    normed_query = normalize(query_rows, gain_query)
    normed_key = normalize(key_rows, gain_key)
    key_all = normed_key.reshape(FRAMES * FTOK, HEADS, HD).astype(jnp.float32)
    value_all = value_rows.reshape(FRAMES * FTOK, HEADS, HD).astype(jnp.float32)
    key_rank = jnp.repeat(slot_order.astype(jnp.int32), FTOK)
    score_scale = HD ** (-0.5)

    def attend_frame(inputs):
        frame_query, frame_rank = inputs
        query_heads = frame_query.reshape(FTOK, HEADS, HD).astype(jnp.float32)
        scores = jnp.einsum('qhd,khd->qhk', query_heads, key_all) * score_scale
        visible = (key_rank <= frame_rank)[None, None, :]
        masked = jnp.where(visible, scores, -1e+30)
        top = lax.optimization_barrier(jnp.max(masked, axis=-1))
        exponent = jnp.where(visible, jnp.exp(masked - top[..., None]), 0.0)
        total = lax.optimization_barrier(jnp.sum(exponent, axis=-1))
        weights = exponent.astype(jnp.bfloat16).astype(jnp.float32)
        summed = jnp.einsum('qhk,khd->qhd', weights, value_all)
        return (summed / total[..., None]).astype(jnp.bfloat16).reshape(FTOK, QK)
    attended = lax.map(attend_frame, (normed_query, slot_order.astype(jnp.int32)))
    group_width = QK // N_SEQ
    attended_groups = attended.reshape(FRAMES * FTOK, N_SEQ, group_width).transpose(1, 0, 2)
    weight_groups = out_weight.reshape(N_SEQ, group_width, D)

    def add_group(carry, pieces):
        attended_piece, weight_piece = pieces
        term = jnp.dot(attended_piece, weight_piece, preferred_element_type=jnp.float32)
        return (carry + term.astype(jnp.bfloat16).astype(jnp.float32), None)
    projected, unused = lax.scan(add_group, jnp.zeros((FRAMES * FTOK, D), jnp.float32), (attended_groups, weight_groups))
    projected = projected.reshape(FRAMES, FTOK, D)
    gate_rows = gate_table[noise_level.astype(jnp.int32)].astype(jnp.float32)
    mixed = tokens.astype(jnp.float32) + gate_rows[:, None, :] * (projected + out_bias.astype(jnp.float32))
    return mixed.astype(jnp.bfloat16)
```

```python
import functools

import jax
import jax.numpy as jnp
from jax import lax
from jax.experimental import pallas as pl
from jax.experimental.pallas import tpu as pltpu
from jax.sharding import PartitionSpec as P

HD = 128
EPS = 1e-06
X, Y, Z = 4, 4, 8
ROWS = 32
GROUP = X * Z * ROWS
D = 5120
HALF = D // 2
SUBS = 2
SUB = HALF // SUBS
MESH = pl.DeviceIdType.MESH
LOG2E = 1.4426950408889634


def position():
    frame = lax.axis_index("frame")
    seq = lax.axis_index("seq")
    return lax.rem(frame, X), frame // X, seq // 2, lax.rem(seq, 2)


def device(x, y, z, c):
    return (y * X + x, z * 2 + c)


def remote(src, dst, send, recv, dev):
    return pltpu.make_async_remote_copy(
        src_ref=src, dst_ref=dst, send_sem=send, recv_sem=recv, device_id=dev, device_id_type=MESH
    )


def plane_peer(d, x, z):
    return lax.rem(x + lax.rem(d, X), X), lax.rem(z + d // X, Z)


def normalize_into(rows_ref, gain_ref, out_ref):
    values = rows_ref[...].astype(jnp.float32)
    inverse = lax.rsqrt(jnp.mean(values * values, axis=-1, keepdims=True) + EPS)
    for h in range(rows_ref.shape[1] // HD):
        part = rows_ref[:, h * HD : (h + 1) * HD].astype(jnp.float32)
        out_ref[h] = (part * inverse * gain_ref[:, h * HD : (h + 1) * HD]).astype(jnp.bfloat16)


def gather_kernel(
    q_ref, k_ref, v_ref, gq_ref, gk_ref, w_ref,
    qo, ko, vo, wo,
    qn, kn,
    a2a_send, a2a_recv, own_sem,
    near_send, near_recv, far_send, far_recv, swap_send, swap_recv, w_sem,
):
    x, y, z, c = position()
    up, down = lax.rem(y + 1, Y), lax.rem(y + Y - 1, Y)
    opposite = lax.rem(y + 2, Y)
    partner = device(x, y, z, 1 - c)
    dev_up, dev_down = device(x, up, z, c), device(x, down, z, c)

    barrier = pltpu.get_barrier_semaphore()

    def greet(i, carry):
        tx, tz = plane_peer(i + 1, x, z)
        pl.semaphore_signal(barrier, inc=1, device_id=device(tx, y, tz, c), device_id_type=MESH)
        return carry

    lax.fori_loop(0, X * Z - 1, greet, 0)
    for dev in (dev_up, dev_down, partner):
        pl.semaphore_signal(barrier, inc=1, device_id=dev, device_id_type=MESH)
    w_own = pltpu.make_async_copy(w_ref, wo.at[c], w_sem.at[0])
    w_own.start()
    normalize_into(k_ref, gk_ref, kn)
    pl.semaphore_wait(barrier, X * Z - 1 + 3)

    slot = pl.ds((x * Z + z) * ROWS, ROWS)

    def scatter(kind, source, target):
        def send(i, carry):
            tx, tz = plane_peer(i + 1, x, z)
            remote(
                source(tz * X + tx), target, a2a_send.at[kind], a2a_recv.at[kind], device(tx, y, tz, c)
            ).start()
            return carry

        lax.fori_loop(0, X * Z - 1, send, 0)
        own = pltpu.make_async_copy(source(z * X + x), target, own_sem.at[kind])
        own.start()
        return own

    def arrived(kind, whole):
        part = whole.at[pl.ds(0, GROUP - ROWS)]
        pltpu.make_async_copy(part, part, a2a_recv.at[kind]).wait()

    own_k = scatter(0, lambda h: kn.at[h], ko.at[c, y, slot])
    own_v = scatter(1, lambda h: v_ref.at[:, pl.ds(h * HD, HD)], vo.at[c, y, slot])
    normalize_into(q_ref, gq_ref, qn)
    own_q = scatter(2, lambda h: qn.at[h], qo.at[slot])
    w_swap = remote(w_ref, wo.at[c], w_sem.at[1], w_sem.at[2], partner)
    w_swap.start()

    pending = []
    half = GROUP // 2
    near = {}
    for t, (buf, own) in enumerate(((ko, own_k), (vo, own_v))):
        own.wait()
        arrived(t, buf.at[c, y])
        mine = buf.at[c, y]
        near[t] = (
            remote(mine, mine, near_send.at[t, 0], near_recv.at[t, 0], dev_up),
            remote(mine, mine, near_send.at[t, 1], near_recv.at[t, 1], dev_down),
        )
        for copy in near[t]:
            copy.start()
        swap = remote(mine, mine, swap_send.at[t, 0], swap_recv.at[t, 0], partner)
        swap.start()
        pending.append(swap)
    far = {}
    for t, buf in enumerate((ko, vo)):
        lower, upper = buf.at[c, down], buf.at[c, up]
        near[t][0].wait_recv()
        first = lower.at[pl.ds(0, half)]
        go_up = remote(first, first, far_send.at[t, 0], far_recv.at[t, 0], dev_up)
        go_up.start()
        near[t][1].wait_recv()
        second = upper.at[pl.ds(half, half)]
        go_down = remote(second, second, far_send.at[t, 1], far_recv.at[t, 1], dev_down)
        go_down.start()
        far[t] = (go_up, go_down)
        for i, block in ((1, lower), (2, upper)):
            swap = remote(block, block, swap_send.at[t, i], swap_recv.at[t, i], partner)
            swap.start()
            pending.append(swap)
    for t, buf in enumerate((ko, vo)):
        far[t][0].wait_recv()
        far[t][1].wait_recv()
        block = buf.at[c, opposite]
        swap = remote(block, block, swap_send.at[t, 3], swap_recv.at[t, 3], partner)
        swap.start()
        pending.append(swap)
    own_q.wait()
    arrived(2, qo)
    w_own.wait()
    w_swap.wait()
    for copy in pending:
        copy.wait()
    for t in range(2):
        for copy in near[t] + far[t]:
            copy.wait_send()
    for kind, whole in enumerate((ko.at[c, y], vo.at[c, y], qo)):
        part = whole.at[pl.ds(0, GROUP - ROWS)]
        pltpu.make_async_copy(part, part, a2a_send.at[kind]).wait()


def attend_kernel(order_ref, count_ref, q_ref, k_ref, v_ref, o_ref, s_ref, m_ref, l_ref, acc_ref):
    frame = lax.axis_index("frame")
    y = frame // X
    scale = (HD ** -0.5) * LOG2E
    rows = GROUP // X

    def block(ref, c, f):
        start = pl.multiple_of(lax.rem(f, X) * rows, rows)
        return ref[c, f // X, pl.ds(start, rows), :]

    def one_query_frame(g, carry):
        start = pl.multiple_of(g * rows, rows)
        query = q_ref[pl.ds(start, rows), :]
        visible = count_ref[y * X + g]
        m_ref[...] = jnp.full_like(m_ref, -jnp.inf)
        l_ref[...] = jnp.zeros_like(l_ref)
        acc_ref[...] = jnp.zeros_like(acc_ref)

        def score(j, carry):
            f = order_ref[j]
            best = m_ref[...]
            for c in range(2):
                s = lax.dot_general(
                    query, block(k_ref, c, f), (((1,), (1,)), ((), ())),
                    preferred_element_type=jnp.float32,
                )
                s_ref[j * 2 + c] = s
                for i in range(rows // 128):
                    best = jnp.maximum(best, s[:, i * 128 : (i + 1) * 128])
            m_ref[...] = best
            return carry

        lax.fori_loop(0, visible, score, 0)
        top = jnp.max(m_ref[...], axis=-1, keepdims=True) * scale

        def weigh(j, carry):
            f = order_ref[j]
            for c in range(2):
                e = jnp.exp2(s_ref[j * 2 + c] * scale - top)
                total = l_ref[...]
                for i in range(rows // 128):
                    total = total + e[:, i * 128 : (i + 1) * 128]
                l_ref[...] = total
                acc_ref[...] += jnp.dot(
                    e.astype(jnp.bfloat16), block(v_ref, c, f), preferred_element_type=jnp.float32
                )
            return carry

        lax.fori_loop(0, visible, weigh, 0)
        total = jnp.sum(l_ref[...], axis=-1, keepdims=True)
        o_ref[pl.ds(start, rows), :] = (acc_ref[...] / total).astype(jnp.bfloat16)
        return carry

    lax.fori_loop(0, X, one_query_frame, 0)


def project_kernel(
    att_ref, w_hbm, tok_ref, bias_ref, gate_ref, level_ref,
    out_ref,
    w_ref, a_ref, part, held,
    w_sem, x_send, x_recv, own_sem, ring_send, ring_recv,
):
    x, y, z, c = position()
    up, down = device(x, y, lax.rem(z + 1, Z), c), device(x, y, lax.rem(z + Z - 1, Z), c)
    barrier = pltpu.get_barrier_semaphore()
    others = [device(lax.rem(x + d, X), y, z, c) for d in range(1, X)]
    for dev in others + [up, down]:
        pl.semaphore_signal(barrier, inc=1, device_id=dev, device_id_type=MESH)
    loads = [pltpu.make_async_copy(w_hbm.at[i], w_ref.at[pl.ds(i * 256, 256)], w_sem.at[i]) for i in range(2)]
    for load in loads:
        load.start()
    pl.semaphore_wait(barrier, len(others) + 2)
    rows = GROUP // X
    columns = pl.ds(pl.multiple_of(x * HD, HD), HD)
    sends = []
    for d in range(1, X):
        tx = lax.rem(x + d, X)
        sends.append(
            remote(
                att_ref.at[pl.ds(tx * rows, rows)], a_ref.at[:, columns],
                x_send.at[d - 1], x_recv.at[d - 1], others[d - 1],
            )
        )
        sends[-1].start()
    own = pltpu.make_async_copy(att_ref.at[pl.ds(x * rows, rows)], a_ref.at[:, columns], own_sem)
    own.start()
    own.wait()
    for load in loads:
        load.wait()
    for copy in sends:
        copy.wait()

    def chunk_rows(index):
        return pl.ds(pl.multiple_of(index * ROWS, ROWS), ROWS)

    def ring(way, sub, step):
        where = pl.ds((way * SUBS + sub) * SUB, SUB)
        if step == 0:
            chunk = lax.rem(z + Z - 1, Z) if way == 0 else lax.rem(z + 1, Z)
            source = part.at[chunk_rows(chunk), where]
        else:
            source = held.at[step - 1, :, where]
        at = (way * SUBS + sub, step)
        return remote(
            source, held.at[step, :, where], ring_send.at[at], ring_recv.at[at], up if way == 0 else down
        )

    copies = {}
    order = [(way, sub) for sub in range(SUBS) for way in range(2)]
    for way, sub in order:
        base = (way * SUBS + sub) * SUB
        tile = SUB // 2

        @pl.loop(0, 2)
        def _(i):
            at = pl.ds(pl.multiple_of(base + i * tile, 128), tile)
            part[:, at] = jnp.dot(
                a_ref[...], w_ref[:, at], preferred_element_type=jnp.float32
            ).astype(jnp.bfloat16)

        copies[way, sub, 0] = ring(way, sub, 0)
        copies[way, sub, 0].start()
    last = Z - 2
    for step in range(1, Z - 1):
        for way, sub in order:
            copies[way, sub, step - 1].wait_recv()
            where = pl.ds((way * SUBS + sub) * SUB, SUB)
            chunk = lax.rem(z + 2 * Z - 1 - step, Z) if way == 0 else lax.rem(z + 1 + step, Z)
            mine = part[chunk_rows(chunk), where].astype(jnp.float32)
            held[step - 1, :, where] = (held[step - 1, :, where].astype(jnp.float32) + mine).astype(
                jnp.bfloat16
            )
            copies[way, sub, step] = ring(way, sub, step)
            copies[way, sub, step].start()
    level = level_ref[lax.axis_index("frame")]
    hot = (lax.broadcasted_iota(jnp.int32, (8, gate_ref.shape[0]), 1) == level).astype(jnp.bfloat16)
    for way, sub in order:
        copies[way, sub, last].wait_recv()
        where = pl.ds((way * SUBS + sub) * SUB, SUB)
        gate = jnp.dot(hot, gate_ref[:, where], preferred_element_type=jnp.float32)[0:1]
        mine = part[chunk_rows(z), where].astype(jnp.float32)
        projected = held[last, :, where].astype(jnp.float32) + mine
        mixed = tok_ref[:, where].astype(jnp.float32) + gate * (
            projected + bias_ref[:, where].astype(jnp.float32)
        )
        out_ref[:, where] = mixed.astype(jnp.bfloat16)
    for copy in copies.values():
        copy.wait_send()


def shards(
    tokens, query_rows, key_rows, value_rows, gain_query, gain_key,
    out_weight, out_bias, gate_table, noise_level, slot_order,
):
    vmem = pl.BlockSpec(memory_space=pltpu.VMEM)
    hbm = pl.BlockSpec(memory_space=pl.ANY)
    smem = pl.BlockSpec(memory_space=pltpu.SMEM)
    bf16 = jnp.bfloat16
    dma = pltpu.SemaphoreType.DMA
    kv = jax.ShapeDtypeStruct((2, Y, GROUP, HD), bf16)
    q, k, v, w = pl.pallas_call(
        gather_kernel,
        out_shape=(
            jax.ShapeDtypeStruct((GROUP, HD), bf16), kv, kv,
            jax.ShapeDtypeStruct((2,) + out_weight.shape, bf16),
        ),
        in_specs=[vmem] * 5 + [hbm],
        out_specs=(hbm,) * 4,
        scratch_shapes=[
            pltpu.VMEM((X * Z, ROWS, HD), bf16),
            pltpu.VMEM((X * Z, ROWS, HD), bf16),
            dma((3,)), dma((3,)), dma((3,)),
            dma((2, 2)), dma((2, 2)), dma((2, 2)), dma((2, 2)), dma((2, 4)), dma((2, 4)), dma((3,)),
        ],
        compiler_params=pltpu.CompilerParams(collective_id=0, has_side_effects=True),
        name="gather",
    )(
        query_rows[0], key_rows[0], value_rows[0],
        gain_query[None].astype(jnp.float32), gain_key[None].astype(jnp.float32), out_weight,
    )
    stamps = slot_order.astype(jnp.int32)
    earlier = (stamps[None, :] <= stamps[:, None]).astype(jnp.int32)
    count = jnp.sum(earlier, axis=1)
    ids = jnp.arange(stamps.shape[0], dtype=jnp.int32)
    order = jnp.sum(jnp.where(count[None, :] == ids[:, None] + 1, ids[None, :], 0), axis=1)
    rows = GROUP // X
    attended = pl.pallas_call(
        attend_kernel,
        out_shape=jax.ShapeDtypeStruct((GROUP, HD), bf16),
        in_specs=[smem, smem, vmem, vmem, vmem],
        out_specs=vmem,
        scratch_shapes=[
            pltpu.VMEM((32, rows, rows), jnp.float32),
            pltpu.VMEM((rows, 128), jnp.float32),
            pltpu.VMEM((rows, 128), jnp.float32),
            pltpu.VMEM((rows, HD), jnp.float32),
        ],
        compiler_params=pltpu.CompilerParams(vmem_limit_bytes=40 * 2**20),
        name="attend",
    )(order, count, q, k, v)
    out = pl.pallas_call(
        project_kernel,
        out_shape=jax.ShapeDtypeStruct((ROWS, D), bf16),
        in_specs=[hbm, hbm, vmem, vmem, vmem, smem],
        out_specs=vmem,
        scratch_shapes=[
            pltpu.VMEM((512, D), bf16),
            pltpu.VMEM((rows, 512), bf16),
            pltpu.VMEM((rows, D), bf16),
            pltpu.VMEM((Z - 1, ROWS, D), bf16),
            dma((2,)), dma((3,)), dma((3,)), dma(()), dma((2 * SUBS, Z - 1)), dma((2 * SUBS, Z - 1)),
        ],
        compiler_params=pltpu.CompilerParams(
            collective_id=1, has_side_effects=True, vmem_limit_bytes=48 * 2**20
        ),
        name="project",
    )(attended, w, tokens[0], out_bias[None], gate_table, noise_level.astype(jnp.int32))
    return out[None]


def solution(mesh):
    placed = (
        P("frame", "seq", None), P("frame", "seq", None), P("frame", "seq", None), P("frame", "seq", None),
        P(), P(), P("seq", None), P(), P(), P(), P(),
    )
    return jax.shard_map(
        shards, mesh=mesh, in_specs=placed, out_specs=P("frame", "seq", None), check_vma=False
    )
```

```python
import functools

import jax
import jax.numpy as jnp
from jax import lax
from jax.experimental import pallas as pl
from jax.experimental.pallas import tpu as pltpu
from jax.sharding import PartitionSpec as P

HD = 128
EPS = 1e-06
X, Y, Z = 4, 4, 8
ROWS = 32
GROUP = X * Z * ROWS
D = 5120
HALF = D // 2
SUBS = 2
SUB = HALF // SUBS
MESH = pl.DeviceIdType.MESH
LOG2E = 1.4426950408889634


def position():
    frame = lax.axis_index("frame")
    seq = lax.axis_index("seq")
    return lax.rem(frame, X), frame // X, seq // 2, lax.rem(seq, 2)


def device(x, y, z, c):
    return (y * X + x, z * 2 + c)


def remote(src, dst, send, recv, dev):
    return pltpu.make_async_remote_copy(
        src_ref=src, dst_ref=dst, send_sem=send, recv_sem=recv, device_id=dev, device_id_type=MESH
    )


def plane_peer(d, x, z):
    return lax.rem(x + lax.rem(d, X), X), lax.rem(z + d // X, Z)


def normalize_into(rows_ref, gain_ref, out_ref):
    values = rows_ref[...].astype(jnp.float32)
    inverse = lax.rsqrt(jnp.mean(values * values, axis=-1, keepdims=True) + EPS)
    for h in range(rows_ref.shape[1] // HD):
        part = rows_ref[:, h * HD : (h + 1) * HD].astype(jnp.float32)
        out_ref[h] = (part * inverse * gain_ref[:, h * HD : (h + 1) * HD]).astype(jnp.bfloat16)


def gather_kernel(
    q_ref, k_ref, v_ref, gq_ref, gk_ref, w_ref,
    qo, ko, vo, wo,
    qn, kn,
    a2a_send, a2a_recv, own_sem,
    near_send, near_recv, far_send, far_recv, swap_send, swap_recv, w_sem,
):
    x, y, z, c = position()
    up, down = lax.rem(y + 1, Y), lax.rem(y + Y - 1, Y)
    opposite = lax.rem(y + 2, Y)
    partner = device(x, y, z, 1 - c)
    dev_up, dev_down = device(x, up, z, c), device(x, down, z, c)

    barrier = pltpu.get_barrier_semaphore()

    def greet(i, carry):
        tx, tz = plane_peer(i + 1, x, z)
        pl.semaphore_signal(barrier, inc=1, device_id=device(tx, y, tz, c), device_id_type=MESH)
        return carry

    lax.fori_loop(0, X * Z - 1, greet, 0)
    for dev in (dev_up, dev_down, partner):
        pl.semaphore_signal(barrier, inc=1, device_id=dev, device_id_type=MESH)
    normalize_into(k_ref, gk_ref, kn)
    pl.semaphore_wait(barrier, X * Z - 1 + 3)

    slot = pl.ds((x * Z + z) * ROWS, ROWS)

    def scatter(kind, source, target):
        def send(i, carry):
            tx, tz = plane_peer(i + 1, x, z)
            remote(
                source(tz * X + tx), target, a2a_send.at[kind], a2a_recv.at[kind], device(tx, y, tz, c)
            ).start()
            return carry

        lax.fori_loop(0, X * Z - 1, send, 0)
        own = pltpu.make_async_copy(source(z * X + x), target, own_sem.at[kind])
        own.start()
        return own

    def arrived(kind, whole):
        part = whole.at[pl.ds(0, GROUP - ROWS)]
        pltpu.make_async_copy(part, part, a2a_recv.at[kind]).wait()

    own_k = scatter(0, lambda h: kn.at[h], ko.at[c, y, slot])
    own_v = scatter(1, lambda h: v_ref.at[:, pl.ds(h * HD, HD)], vo.at[c, y, slot])
    normalize_into(q_ref, gq_ref, qn)
    own_q = scatter(2, lambda h: qn.at[h], qo.at[slot])
    w_swap = remote(w_ref, wo, w_sem.at[0], w_sem.at[1], partner)
    w_swap.start()

    pending = []
    half = GROUP // 2
    near = {}
    for t, (buf, own) in enumerate(((ko, own_k), (vo, own_v))):
        own.wait()
        arrived(t, buf.at[c, y])
        mine = buf.at[c, y]
        near[t] = (
            remote(mine, mine, near_send.at[t, 0], near_recv.at[t, 0], dev_up),
            remote(mine, mine, near_send.at[t, 1], near_recv.at[t, 1], dev_down),
        )
        for copy in near[t]:
            copy.start()
        swap = remote(mine, mine, swap_send.at[t, 0], swap_recv.at[t, 0], partner)
        swap.start()
        pending.append(swap)
    far = {}
    for t, buf in enumerate((ko, vo)):
        lower, upper = buf.at[c, down], buf.at[c, up]
        near[t][0].wait_recv()
        first = lower.at[pl.ds(0, half)]
        go_up = remote(first, first, far_send.at[t, 0], far_recv.at[t, 0], dev_up)
        go_up.start()
        near[t][1].wait_recv()
        second = upper.at[pl.ds(half, half)]
        go_down = remote(second, second, far_send.at[t, 1], far_recv.at[t, 1], dev_down)
        go_down.start()
        far[t] = (go_up, go_down)
        for i, block in ((1, lower), (2, upper)):
            swap = remote(block, block, swap_send.at[t, i], swap_recv.at[t, i], partner)
            swap.start()
            pending.append(swap)
    for t, buf in enumerate((ko, vo)):
        far[t][0].wait_recv()
        far[t][1].wait_recv()
        block = buf.at[c, opposite]
        swap = remote(block, block, swap_send.at[t, 3], swap_recv.at[t, 3], partner)
        swap.start()
        pending.append(swap)
    own_q.wait()
    arrived(2, qo)
    w_swap.wait()
    for copy in pending:
        copy.wait()
    for t in range(2):
        for copy in near[t] + far[t]:
            copy.wait_send()
    for kind, whole in enumerate((ko.at[c, y], vo.at[c, y], qo)):
        part = whole.at[pl.ds(0, GROUP - ROWS)]
        pltpu.make_async_copy(part, part, a2a_send.at[kind]).wait()


def attend_kernel(order_ref, count_ref, q_ref, k_ref, v_ref, o_ref, s_ref, m_ref, l_ref, acc_ref):
    frame = lax.axis_index("frame")
    y = frame // X
    scale = (HD ** -0.5) * LOG2E
    rows = GROUP // X

    def block(ref, c, f):
        start = pl.multiple_of(lax.rem(f, X) * rows, rows)
        return ref[c, f // X, pl.ds(start, rows), :]

    def one_query_frame(g, carry):
        start = pl.multiple_of(g * rows, rows)
        query = q_ref[pl.ds(start, rows), :]
        visible = count_ref[y * X + g]
        m_ref[...] = jnp.full_like(m_ref, -jnp.inf)
        l_ref[...] = jnp.zeros_like(l_ref)
        acc_ref[...] = jnp.zeros_like(acc_ref)

        def score(j, carry):
            f = order_ref[j]
            best = m_ref[...]
            for c in range(2):
                s = lax.dot_general(
                    query, block(k_ref, c, f), (((1,), (1,)), ((), ())),
                    preferred_element_type=jnp.float32,
                )
                s_ref[j * 2 + c] = s
                for i in range(rows // 128):
                    best = jnp.maximum(best, s[:, i * 128 : (i + 1) * 128])
            m_ref[...] = best
            return carry

        lax.fori_loop(0, visible, score, 0)
        top = jnp.max(m_ref[...], axis=-1, keepdims=True) * scale

        def weigh(j, carry):
            f = order_ref[j]
            for c in range(2):
                e = jnp.exp2(s_ref[j * 2 + c] * scale - top)
                total = l_ref[...]
                for i in range(rows // 128):
                    total = total + e[:, i * 128 : (i + 1) * 128]
                l_ref[...] = total
                acc_ref[...] += jnp.dot(
                    e.astype(jnp.bfloat16), block(v_ref, c, f), preferred_element_type=jnp.float32
                )
            return carry

        lax.fori_loop(0, visible, weigh, 0)
        total = jnp.sum(l_ref[...], axis=-1, keepdims=True)
        o_ref[pl.ds(start, rows), :] = (acc_ref[...] / total).astype(jnp.bfloat16)
        return carry

    lax.fori_loop(0, X, one_query_frame, 0)


def project_kernel(
    att_ref, w_own, w_other, tok_ref, bias_ref, gate_ref, level_ref,
    out_ref,
    w_ref, a_ref, part, held,
    w_sem, x_send, x_recv, own_sem, ring_send, ring_recv,
):
    x, y, z, c = position()
    up, down = device(x, y, lax.rem(z + 1, Z), c), device(x, y, lax.rem(z + Z - 1, Z), c)
    barrier = pltpu.get_barrier_semaphore()
    others = [device(lax.rem(x + d, X), y, z, c) for d in range(1, X)]
    for dev in others + [up, down]:
        pl.semaphore_signal(barrier, inc=1, device_id=dev, device_id_type=MESH)
    loads = [
        pltpu.make_async_copy(
            source, w_ref.at[pl.ds(pl.multiple_of(core * 256, 256), 256)], w_sem.at[i]
        )
        for i, (source, core) in enumerate(((w_own, c), (w_other, 1 - c)))
    ]
    for load in loads:
        load.start()
    pl.semaphore_wait(barrier, len(others) + 2)
    rows = GROUP // X
    columns = pl.ds(pl.multiple_of(x * HD, HD), HD)
    sends = []
    for d in range(1, X):
        tx = lax.rem(x + d, X)
        sends.append(
            remote(
                att_ref.at[pl.ds(tx * rows, rows)], a_ref.at[:, columns],
                x_send.at[d - 1], x_recv.at[d - 1], others[d - 1],
            )
        )
        sends[-1].start()
    own = pltpu.make_async_copy(att_ref.at[pl.ds(x * rows, rows)], a_ref.at[:, columns], own_sem)
    own.start()
    own.wait()
    for load in loads:
        load.wait()
    for copy in sends:
        copy.wait()

    def chunk_rows(index):
        return pl.ds(pl.multiple_of(index * ROWS, ROWS), ROWS)

    def ring(way, sub, step):
        where = pl.ds((way * SUBS + sub) * SUB, SUB)
        if step == 0:
            chunk = lax.rem(z + Z - 1, Z) if way == 0 else lax.rem(z + 1, Z)
            source = part.at[chunk_rows(chunk), where]
        else:
            source = held.at[step - 1, :, where]
        at = (way * SUBS + sub, step)
        return remote(
            source, held.at[step, :, where], ring_send.at[at], ring_recv.at[at], up if way == 0 else down
        )

    copies = {}
    order = [(way, sub) for sub in range(SUBS) for way in range(2)]
    for way, sub in order:
        base = (way * SUBS + sub) * SUB
        tile = SUB // 2

        @pl.loop(0, 2)
        def _(i):
            at = pl.ds(pl.multiple_of(base + i * tile, 128), tile)
            part[:, at] = jnp.dot(
                a_ref[...], w_ref[:, at], preferred_element_type=jnp.float32
            ).astype(jnp.bfloat16)

        copies[way, sub, 0] = ring(way, sub, 0)
        copies[way, sub, 0].start()
    last = Z - 2
    for step in range(1, Z - 1):
        for way, sub in order:
            copies[way, sub, step - 1].wait_recv()
            where = pl.ds((way * SUBS + sub) * SUB, SUB)
            chunk = lax.rem(z + 2 * Z - 1 - step, Z) if way == 0 else lax.rem(z + 1 + step, Z)
            mine = part[chunk_rows(chunk), where].astype(jnp.float32)
            held[step - 1, :, where] = (held[step - 1, :, where].astype(jnp.float32) + mine).astype(
                jnp.bfloat16
            )
            copies[way, sub, step] = ring(way, sub, step)
            copies[way, sub, step].start()
    level = level_ref[lax.axis_index("frame")]
    hot = (lax.broadcasted_iota(jnp.int32, (8, gate_ref.shape[0]), 1) == level).astype(jnp.bfloat16)
    for way, sub in order:
        copies[way, sub, last].wait_recv()
        where = pl.ds((way * SUBS + sub) * SUB, SUB)
        gate = jnp.dot(hot, gate_ref[:, where], preferred_element_type=jnp.float32)[0:1]
        mine = part[chunk_rows(z), where].astype(jnp.float32)
        projected = held[last, :, where].astype(jnp.float32) + mine
        mixed = tok_ref[:, where].astype(jnp.float32) + gate * (
            projected + bias_ref[:, where].astype(jnp.float32)
        )
        out_ref[:, where] = mixed.astype(jnp.bfloat16)
    for copy in copies.values():
        copy.wait_send()


def shards(
    tokens, query_rows, key_rows, value_rows, gain_query, gain_key,
    out_weight, out_bias, gate_table, noise_level, slot_order,
):
    vmem = pl.BlockSpec(memory_space=pltpu.VMEM)
    hbm = pl.BlockSpec(memory_space=pl.ANY)
    smem = pl.BlockSpec(memory_space=pltpu.SMEM)
    bf16 = jnp.bfloat16
    dma = pltpu.SemaphoreType.DMA
    kv = jax.ShapeDtypeStruct((2, Y, GROUP, HD), bf16)
    q, k, v, w = pl.pallas_call(
        gather_kernel,
        out_shape=(
            jax.ShapeDtypeStruct((GROUP, HD), bf16), kv, kv,
            jax.ShapeDtypeStruct(out_weight.shape, bf16),
        ),
        in_specs=[vmem] * 5 + [hbm],
        out_specs=(hbm,) * 4,
        scratch_shapes=[
            pltpu.VMEM((X * Z, ROWS, HD), bf16),
            pltpu.VMEM((X * Z, ROWS, HD), bf16),
            dma((3,)), dma((3,)), dma((3,)),
            dma((2, 2)), dma((2, 2)), dma((2, 2)), dma((2, 2)), dma((2, 4)), dma((2, 4)), dma((2,)),
        ],
        compiler_params=pltpu.CompilerParams(collective_id=0, has_side_effects=True),
        name="gather",
    )(
        query_rows[0], key_rows[0], value_rows[0],
        gain_query[None].astype(jnp.float32), gain_key[None].astype(jnp.float32), out_weight,
    )
    stamps = slot_order.astype(jnp.int32)
    earlier = (stamps[None, :] <= stamps[:, None]).astype(jnp.int32)
    count = jnp.sum(earlier, axis=1)
    ids = jnp.arange(stamps.shape[0], dtype=jnp.int32)
    order = jnp.sum(jnp.where(count[None, :] == ids[:, None] + 1, ids[None, :], 0), axis=1)
    rows = GROUP // X
    attended = pl.pallas_call(
        attend_kernel,
        out_shape=jax.ShapeDtypeStruct((GROUP, HD), bf16),
        in_specs=[smem, smem, vmem, vmem, vmem],
        out_specs=vmem,
        scratch_shapes=[
            pltpu.VMEM((32, rows, rows), jnp.float32),
            pltpu.VMEM((rows, 128), jnp.float32),
            pltpu.VMEM((rows, 128), jnp.float32),
            pltpu.VMEM((rows, HD), jnp.float32),
        ],
        compiler_params=pltpu.CompilerParams(vmem_limit_bytes=40 * 2**20),
        name="attend",
    )(order, count, q, k, v)
    out = pl.pallas_call(
        project_kernel,
        out_shape=jax.ShapeDtypeStruct((ROWS, D), bf16),
        in_specs=[hbm, hbm, hbm, vmem, vmem, vmem, smem],
        out_specs=vmem,
        scratch_shapes=[
            pltpu.VMEM((512, D), bf16),
            pltpu.VMEM((rows, 512), bf16),
            pltpu.VMEM((rows, D), bf16),
            pltpu.VMEM((Z - 1, ROWS, D), bf16),
            dma((2,)), dma((3,)), dma((3,)), dma(()), dma((2 * SUBS, Z - 1)), dma((2 * SUBS, Z - 1)),
        ],
        compiler_params=pltpu.CompilerParams(
            collective_id=1, has_side_effects=True, vmem_limit_bytes=48 * 2**20
        ),
        name="project",
    )(attended, out_weight, w, tokens[0], out_bias[None], gate_table, noise_level.astype(jnp.int32))
    return out[None]


def solution(mesh):
    placed = (
        P("frame", "seq", None), P("frame", "seq", None), P("frame", "seq", None), P("frame", "seq", None),
        P(), P(), P("seq", None), P(), P(), P(), P(),
    )
    return jax.shard_map(
        shards, mesh=mesh, in_specs=placed, out_specs=P("frame", "seq", None), check_vma=False
    )
```

```python
import functools

import jax
import jax.numpy as jnp
from jax import lax
from jax.experimental import pallas as pl
from jax.experimental.pallas import tpu as pltpu
from jax.sharding import PartitionSpec as P

HD = 128
EPS = 1e-06
X, Y, Z = 4, 4, 8
ROWS = 32
HALVES = 2
HROWS = ROWS // HALVES
QROWS = X * Z * HROWS
FROWS = Z * HROWS
GROUP = X * Z * ROWS
KROWS = Z * ROWS
D = 5120
DEPTH = 512
SUBS = 4
SUB = D // SUBS
STEPS = Z // 2
MESH = pl.DeviceIdType.MESH
SCALE = HD ** -0.5 * 1.4426950408889634
HIDDEN = -1e30


def position():
    frame = lax.axis_index("frame")
    seq = lax.axis_index("seq")
    return lax.rem(frame, X), frame // X, seq // 2, lax.rem(seq, 2)


def device(x, y, z, c):
    return (y * X + x, z * 2 + c)


def remote(src, dst, send, recv, dev):
    return pltpu.make_async_remote_copy(
        src_ref=src, dst_ref=dst, send_sem=send, recv_sem=recv, device_id=dev, device_id_type=MESH
    )


def plane_peer(d, x, z):
    return lax.rem(x + lax.rem(d, X), X), lax.rem(z + d // X, Z)


def normalize_into(rows_ref, gain_ref, out_ref):
    values = rows_ref[...].astype(jnp.float32)
    inverse = lax.rsqrt(jnp.mean(values * values, axis=-1, keepdims=True) + EPS)
    for h in range(X * Z):
        at = slice(h * HD, (h + 1) * HD)
        part = (rows_ref[:, at].astype(jnp.float32) * inverse * gain_ref[:, at]).astype(jnp.bfloat16)
        out_ref[h] = part.reshape(out_ref.shape[1:])


def fused_kernel(
    stamp_ref, level_ref, q_ref, k_ref, v_ref, gq_ref, gk_ref, w_hbm, tok_hbm, bias_hbm, gate_hbm,
    out_ref,
    qn, kn, qb, kb, vb, top_ref, sum_ref, acc_ref, att, a_ref, w_ref, part, held, tok_ref, bias_ref, gate_ref,
    a2a_send, a2a_recv, own_sem, near_send, near_recv, far_send, far_recv, swap_send, swap_recv,
    w_sem, load_sem, x_send, x_recv, ring_send, ring_recv,
):
    x, y, z, c = position()
    up, down, opposite = lax.rem(y + 1, Y), lax.rem(y + Y - 1, Y), lax.rem(y + 2, Y)
    partner = device(x, y, z, 1 - c)
    dev_up, dev_down = device(x, up, z, c), device(x, down, z, c)
    next_z, last_z = device(x, y, lax.rem(z + 1, Z), c), device(x, y, lax.rem(z + Z - 1, Z), c)
    groups = (y, down, up, opposite)
    bufs = (kb, vb)

    barrier = pltpu.get_barrier_semaphore()

    def greet(i, carry):
        tx, tz = plane_peer(i + 1, x, z)
        pl.semaphore_signal(barrier, inc=1, device_id=device(tx, y, tz, c), device_id_type=MESH)
        return carry

    lax.fori_loop(0, X * Z - 1, greet, 0)
    for dev in (dev_up, dev_down, partner):
        pl.semaphore_signal(barrier, inc=1, device_id=dev, device_id_type=MESH)
    w_rows = w_ref.at[pl.ds(pl.multiple_of(c * (DEPTH // 2), DEPTH // 2), DEPTH // 2)]
    loads = [
        pltpu.make_async_copy(source, target, load_sem.at[i])
        for i, (source, target) in enumerate(
            ((w_hbm, w_rows), (tok_hbm, tok_ref), (bias_hbm, bias_ref), (gate_hbm, gate_ref))
        )
    ]
    for load in loads:
        load.start()
    normalize_into(k_ref, gk_ref, kn)
    pl.semaphore_wait(barrier, X * Z - 1 + 3)

    slot = pl.ds(pl.multiple_of((x * Z + z) * ROWS, ROWS), ROWS)

    def scatter(kind, source, target):
        def send(i, carry):
            tx, tz = plane_peer(i + 1, x, z)
            remote(
                source(tz * X + tx), target, a2a_send.at[kind], a2a_recv.at[kind], device(tx, y, tz, c)
            ).start()
            return carry

        lax.fori_loop(0, X * Z - 1, send, 0)
        own = pltpu.make_async_copy(source(z * X + x), target, own_sem.at[kind])
        own.start()
        return own

    def all_of(kind, sem):
        rest = kb.at[0, 0, pl.ds(0, GROUP - ROWS)]
        pltpu.make_async_copy(rest, rest, sem.at[kind]).wait()

    own = [
        scatter(0, lambda h: kn.at[h], kb.at[c, y, slot]),
        scatter(1, lambda h: v_ref.at[:, pl.ds(pl.multiple_of(h * HD, HD), HD)], vb.at[c, y, slot]),
    ]
    normalize_into(q_ref, gq_ref, qn)
    own.append(scatter(2, lambda h: qn.at[h], qb.at[x, :, z]))
    w_swap = remote(w_hbm, w_rows, w_sem.at[0], w_sem.at[1], partner)
    w_swap.start()

    half = GROUP // 2

    def near(t, i):
        block = bufs[t].at[c, y]
        return remote(block, block, near_send.at[t, i], near_recv.at[t, i], (dev_up, dev_down)[i])

    def far(t, i):
        block = bufs[t].at[c, (down, up)[i], pl.ds(i * half, half)]
        return remote(block, block, far_send.at[t, i], far_recv.at[t, i], (dev_up, dev_down)[i])

    def swap(t, i):
        block = bufs[t].at[c, groups[i]]
        return remote(block, block, swap_send.at[t, i], swap_recv.at[t, i], partner)

    def pass_own(t):
        own[t].wait()
        all_of(t, a2a_recv)
        near(t, 0).start()
        near(t, 1).start()
        swap(t, 0).start()

    def pass_near(t):
        near(t, 0).wait_recv()
        far(t, 0).start()
        swap(t, 1).start()
        near(t, 1).wait_recv()
        far(t, 1).start()
        swap(t, 2).start()

    def pass_far(t):
        far(t, 0).wait_recv()
        far(t, 1).wait_recv()
        swap(t, 3).start()

    def attend(hh, yy):
        query = qb[:, hh].reshape(QROWS, HD)
        scores = [
            lax.dot_general(
                query, kb[core, yy], (((1,), (1,)), ((), ())), preferred_element_type=jnp.float32
            )
            for core in range(2)
        ]
        key_stamp = [stamp_ref[yy * X + f] for f in range(X)]
        summed = [None, None]
        weights = [[], []]
        alphas = []
        for g in range(X):
            stamp = stamp_ref[y * X + g]
            rows = slice(g * FROWS, (g + 1) * FROWS)
            best = jnp.full((FROWS, 128), 2 * HIDDEN, jnp.float32)
            shift = [jnp.where(key_stamp[f] <= stamp, 0.0, HIDDEN) for f in range(X)]
            for f in range(X):
                seen = None
                for core in range(2):
                    for i in range(f * KROWS, (f + 1) * KROWS, 128):
                        tile = scores[core][rows, i : i + 128]
                        seen = tile if seen is None else jnp.maximum(seen, tile)
                best = jnp.maximum(best, seen + shift[f])
            old = top_ref[hh, rows, :]
            new = jnp.maximum(old, jnp.max(best, axis=-1, keepdims=True) * SCALE)
            alpha = jnp.exp2(old - new)
            top_ref[hh, rows, :] = new
            total = sum_ref[hh, rows, :] * alpha
            column = new[:, 0:1]
            for core in range(2):
                row_weights = []
                for f in range(X):
                    piece = scores[core][rows, f * KROWS : (f + 1) * KROWS]
                    exponent = jnp.exp2(piece * SCALE + (shift[f] - column))
                    for i in range(0, KROWS, 128):
                        total = total + exponent[:, i : i + 128]
                    row_weights.append(exponent.astype(jnp.bfloat16))
                weights[core].append(jnp.concatenate(row_weights, axis=1))
            sum_ref[hh, rows, :] = total
            alphas.append(alpha)
        gained = sum(
            jnp.dot(
                jnp.concatenate(weights[core], axis=0), vb[core, yy], preferred_element_type=jnp.float32
            )
            for core in range(2)
        )
        acc_ref[hh] = acc_ref[hh] * jnp.concatenate(alphas, axis=0) + gained

    def cross(hh, d):
        tx = lax.rem(x + d, X)
        columns = pl.ds(pl.multiple_of(x * HD, HD), HD)
        return remote(
            att.at[hh, tx], a_ref.at[hh, :, columns], x_send.at[hh, d], x_recv.at[hh, d], device(tx, y, z, c)
        )

    def cross_own(hh):
        columns = pl.ds(pl.multiple_of(x * HD, HD), HD)
        return pltpu.make_async_copy(att.at[hh, x], a_ref.at[hh, :, columns], x_send.at[hh, 0])

    def finish(hh):
        total = jnp.sum(sum_ref[hh], axis=-1, keepdims=True)
        att[hh] = (acc_ref[hh] / total).astype(jnp.bfloat16).reshape(X, FROWS, HD)
        for d in range(1, X):
            cross(hh, d).start()
        cross_own(hh).start()

    def chunk(way, step):
        index = lax.rem(z + STEPS - step, Z) if way == 0 else lax.rem(z + STEPS + step, Z)
        return pl.ds(pl.multiple_of(index * HROWS, HROWS), HROWS)

    def opens(way, sub):
        return 0 if sub // (SUBS // 2) == way else 1

    def ring(hh, way, sub, step):
        where = pl.ds(sub * SUB, SUB)
        if step == opens(way, sub):
            source = part.at[hh, chunk(way, step), where]
        else:
            source = held.at[hh, way, step - 1, :, where]
        at = (hh, way, sub, step)
        return remote(
            source, held.at[hh, way, step, :, where], ring_send.at[at], ring_recv.at[at], (next_z, last_z)[way]
        )

    pairs = [(way, sub) for sub in range(SUBS // 2) for way, sub in ((0, sub), (1, sub + SUBS // 2))]
    pairs += [(1 - way, sub) for way, sub in pairs]

    def project(hh):
        for d in range(1, X):
            cross(hh, d).wait_recv()
        cross_own(hh).wait()
        for sub in range(SUBS):
            where = pl.ds(sub * SUB, SUB)
            part[hh, :, where] = jnp.dot(
                a_ref[hh], w_ref[:, where], preferred_element_type=jnp.float32
            ).astype(jnp.bfloat16)
            ring(hh, sub // (SUBS // 2), sub, 0).start()
        for sub in range(SUBS):
            ring(hh, 1 - sub // (SUBS // 2), sub, 1).start()

    def relay(hh, step):
        for way, sub in pairs:
            if step > opens(way, sub):
                ring(hh, way, sub, step - 1).wait_recv()
                where = pl.ds(sub * SUB, SUB)
                mine = part[hh, chunk(way, step), where].astype(jnp.float32)
                came = held[hh, way, step - 1, :, where].astype(jnp.float32)
                held[hh, way, step - 1, :, where] = (came + mine).astype(jnp.bfloat16)
                ring(hh, way, sub, step).start()

    def settle(hh):
        rows = pl.ds(hh * HROWS, HROWS)
        mine_rows = pl.ds(pl.multiple_of(z * HROWS, HROWS), HROWS)
        for sub in range(SUBS):
            where = pl.ds(sub * SUB, SUB)
            projected = part[hh, mine_rows, where].astype(jnp.float32)
            for way in range(2):
                ring(hh, way, sub, STEPS - 1).wait_recv()
                projected = projected + held[hh, way, STEPS - 1, :, where].astype(jnp.float32)
            gate = jnp.dot(hot, gate_ref[:, where], preferred_element_type=jnp.float32)[0:1]
            mixed = tok_ref[rows, where].astype(jnp.float32) + gate * (
                projected + bias_ref[:, where].astype(jnp.float32)
            )
            out_ref[rows, where] = mixed.astype(jnp.bfloat16)

    top_ref[...] = jnp.full_like(top_ref, 2 * HIDDEN)
    sum_ref[...] = jnp.zeros_like(sum_ref)
    acc_ref[...] = jnp.zeros_like(acc_ref)
    pass_own(0)
    pass_own(1)
    pass_near(0)
    own[2].wait()
    all_of(2, a2a_recv)
    pass_far(0)

    def wait_swap(i):
        swap(0, i).wait_recv()
        swap(1, i).wait_recv()

    order = ((0, 0), (0, 1), (0, 2), (1, 0), (0, 3), (1, 1), (1, 2), (1, 3))

    def choose(i, options):
        value = options[0]
        for n in range(1, len(options)):
            value = jnp.where(i == n, options[n], value)
        return value

    def step(i, carry):
        @pl.when(i == 0)
        def _():
            wait_swap(0)

        @pl.when(i == 1)
        def _():
            pass_near(1)
            wait_swap(1)

        @pl.when(i == 2)
        def _():
            wait_swap(2)

        @pl.when(i == 4)
        def _():
            pass_far(1)
            wait_swap(3)

        attend(choose(i, [hh for hh, _ in order]), choose(i, [groups[p] for _, p in order]))

        @pl.when(i == 4)
        def _():
            finish(0)

        @pl.when(i == 5)
        def _():
            for load in loads:
                load.wait()
            w_swap.wait()
            project(0)

        @pl.when(i == 6)
        def _():
            relay(0, 1)

        return carry

    lax.fori_loop(0, len(order), step, 0)
    finish(1)
    relay(0, 2)
    project(1)
    level = level_ref[lax.axis_index("frame")]
    hot = (lax.broadcasted_iota(jnp.int32, (8, gate_ref.shape[0]), 1) == level).astype(jnp.bfloat16)
    relay(0, 3)
    relay(1, 1)
    settle(0)
    relay(1, 2)
    relay(1, 3)
    settle(1)

    for t in range(2):
        for i in range(2):
            near(t, i).wait_send()
            far(t, i).wait_send()
        for i in range(4):
            swap(t, i).wait_send()
    for kind in range(3):
        all_of(kind, a2a_send)
    for hh in range(HALVES):
        for d in range(1, X):
            cross(hh, d).wait_send()
        for way in range(2):
            for sub in range(SUBS):
                for s in range(opens(way, sub), STEPS):
                    ring(hh, way, sub, s).wait_send()


def shards(
    tokens, query_rows, key_rows, value_rows, gain_query, gain_key,
    out_weight, out_bias, gate_table, noise_level, slot_order,
):
    vmem = pl.BlockSpec(memory_space=pltpu.VMEM)
    hbm = pl.BlockSpec(memory_space=pl.ANY)
    smem = pl.BlockSpec(memory_space=pltpu.SMEM)
    bf16, f32 = jnp.bfloat16, jnp.float32
    dma = pltpu.SemaphoreType.DMA
    out = pl.pallas_call(
        fused_kernel,
        out_shape=jax.ShapeDtypeStruct((ROWS, D), bf16),
        in_specs=[smem, smem] + [vmem] * 5 + [hbm] * 4,
        out_specs=vmem,
        scratch_shapes=[
            pltpu.VMEM((X * Z, HALVES, HROWS, HD), bf16),
            pltpu.VMEM((X * Z, ROWS, HD), bf16),
            pltpu.VMEM((X, HALVES, Z, HROWS, HD), bf16),
            pltpu.VMEM((2, Y, GROUP, HD), bf16),
            pltpu.VMEM((2, Y, GROUP, HD), bf16),
            pltpu.VMEM((HALVES, QROWS, 128), f32),
            pltpu.VMEM((HALVES, QROWS, 128), f32),
            pltpu.VMEM((HALVES, QROWS, HD), f32),
            pltpu.VMEM((HALVES, X, FROWS, HD), bf16),
            pltpu.VMEM((HALVES, FROWS, DEPTH), bf16),
            pltpu.VMEM((DEPTH, D), bf16),
            pltpu.VMEM((HALVES, FROWS, D), bf16),
            pltpu.VMEM((HALVES, 2, STEPS, HROWS, D), bf16),
            pltpu.VMEM((ROWS, D), bf16),
            pltpu.VMEM((1, D), bf16),
            pltpu.VMEM(gate_table.shape, bf16),
            dma((3,)), dma((3,)), dma((3,)),
            dma((2, 2)), dma((2, 2)), dma((2, 2)), dma((2, 2)), dma((2, 4)), dma((2, 4)),
            dma((2,)), dma((4,)), dma((HALVES, X)), dma((HALVES, X)),
            dma((HALVES, 2, SUBS, STEPS)), dma((HALVES, 2, SUBS, STEPS)),
        ],
        compiler_params=pltpu.CompilerParams(
            collective_id=0, has_side_effects=True, vmem_limit_bytes=56 * 2**20
        ),
        name="fused",
    )(
        slot_order.astype(jnp.int32), noise_level.astype(jnp.int32),
        query_rows[0], key_rows[0], value_rows[0], gain_query[None], gain_key[None],
        out_weight, tokens[0], out_bias[None], gate_table,
    )
    return out[None]


def solution(mesh):
    placed = (
        P("frame", "seq", None), P("frame", "seq", None), P("frame", "seq", None), P("frame", "seq", None),
        P(), P(), P("seq", None), P(), P(), P(), P(),
    )
    return jax.shard_map(
        shards, mesh=mesh, in_specs=placed, out_specs=P("frame", "seq", None), check_vma=False
    )
```

```python
import functools

import jax
import jax.numpy as jnp
from jax import lax
from jax.experimental import pallas as pl
from jax.experimental.pallas import tpu as pltpu
from jax.sharding import PartitionSpec as P

HD = 128
EPS = 1e-06
X, Y, Z = 4, 4, 8
ROWS = 32
HALVES = 2
HROWS = ROWS // HALVES
QROWS = X * Z * HROWS
FROWS = Z * HROWS
GROUP = X * Z * ROWS
PARTS = 2
PART = GROUP // PARTS
WIDE = X // PARTS
D = 5120
DEPTH = 512
SUBS = 4
SUB = D // SUBS
STEPS = Z // 2
MESH = pl.DeviceIdType.MESH
SCALE = HD ** -0.5 * 1.4426950408889634
HIDDEN = -1e30


def position():
    frame = lax.axis_index("frame")
    seq = lax.axis_index("seq")
    return lax.rem(frame, X), frame // X, seq // 2, lax.rem(seq, 2)


def device(x, y, z, c):
    return (y * X + x, z * 2 + c)


def remote(src, dst, send, recv, dev):
    return pltpu.make_async_remote_copy(
        src_ref=src, dst_ref=dst, send_sem=send, recv_sem=recv, device_id=dev, device_id_type=MESH
    )


def plane_peer(d, x, z):
    return lax.rem(x + lax.rem(d, X), X), lax.rem(z + d // X, Z)


def normalize_into(rows_ref, gain_ref, out_ref):
    values = rows_ref[...].astype(jnp.float32)
    inverse = lax.rsqrt(jnp.mean(values * values, axis=-1, keepdims=True) + EPS)
    for h in range(X * Z):
        at = slice(h * HD, (h + 1) * HD)
        part = (rows_ref[:, at].astype(jnp.float32) * inverse * gain_ref[:, at]).astype(jnp.bfloat16)
        out_ref[h] = part.reshape(out_ref.shape[1:])


def fused_kernel(
    stamp_hbm, level_hbm, q_hbm, k_hbm, v_hbm, gq_hbm, gk_hbm, w_hbm, tok_hbm, bias_hbm, gate_hbm,
    out_ref,
    stamp_ref, level_ref, q_ref, k_ref, gq_ref, gk_ref, qn, kn, qb, kb, vb, top_ref, sum_ref, acc_ref, att, a_ref, w_ref, part, held, tok_ref, bias_ref, gate_ref, bias_row, gate_row,
    a2a_send, a2a_recv, own_sem, near_send, near_recv, far_send, far_recv, swap_send, swap_recv,
    w_sem, load_sem, x_send, x_recv, ring_send, ring_recv,
):
    x, y, z, c = position()
    up, down, opposite = lax.rem(y + 1, Y), lax.rem(y + Y - 1, Y), lax.rem(y + 2, Y)
    partner = device(x, y, z, 1 - c)
    dev_up, dev_down = device(x, up, z, c), device(x, down, z, c)
    next_z, last_z = device(x, y, lax.rem(z + 1, Z), c), device(x, y, lax.rem(z + Z - 1, Z), c)
    groups = (y, down, up, opposite)
    bufs = (vb, kb)

    barrier = pltpu.get_barrier_semaphore()

    def greet(i, carry):
        tx, tz = plane_peer(i + 1, x, z)
        pl.semaphore_signal(barrier, inc=1, device_id=device(tx, y, tz, c), device_id_type=MESH)
        return carry

    lax.fori_loop(0, X * Z - 1, greet, 0)
    for dev in (dev_up, dev_down, partner):
        pl.semaphore_signal(barrier, inc=1, device_id=dev, device_id_type=MESH)
    w_rows = w_ref.at[pl.ds(pl.multiple_of(c * (DEPTH // 2), DEPTH // 2), DEPTH // 2)]
    loads = [
        pltpu.make_async_copy(source, target, load_sem.at[i])
        for i, (source, target) in enumerate(
            (
                (k_hbm, k_ref), (gk_hbm, gk_ref), (q_hbm, q_ref), (gq_hbm, gq_ref),
                (stamp_hbm, stamp_ref), (level_hbm, level_ref), (w_hbm, w_rows), (tok_hbm, tok_ref), (bias_hbm, bias_ref), (gate_hbm, gate_ref),
            )
        )
    ]
    for load in loads:
        load.start()
    pl.semaphore_wait(barrier, X * Z - 1 + 3)

    def scatter(kind, p, first, source, target):
        def send(d, carry):
            dx, dz = first(d)
            tx, tz = lax.rem(x + dx, X), lax.rem(z + dz, Z)
            remote(
                source(tz * X + tx), target(dx), a2a_send.at[kind, p], a2a_recv.at[kind, p],
                device(tx, y, tz, c),
            ).start()
            return carry

        return send

    def zigzag(k):
        return jnp.where(lax.rem(k, 2) == 1, (k + 1) // 2, lax.rem(Z - k // 2, Z))

    def scatter_rows(t, source):
        def target(dx):
            rows = pl.ds(pl.multiple_of((lax.rem(dx, WIDE) * Z + z) * ROWS, ROWS), ROWS)
            return bufs[t].at[c, y, dx // WIDE, rows]

        for p in range(PARTS):
            send = scatter(t, p, lambda d: (p * WIDE + lax.rem(d, WIDE), zigzag(d // WIDE)), source, target)
            lax.fori_loop(1 if p == 0 else 0, WIDE * Z, send, 0)
        own = pltpu.make_async_copy(source(z * X + x), target(0), own_sem.at[t])
        own.start()
        return own

    def scatter_query():
        for hh in range(HALVES):
            send = scatter(
                2, hh, lambda d: (lax.rem(d, X), zigzag(d // X)), lambda h: qn.at[h, hh], lambda dx: qb.at[x, hh, z]
            )
            lax.fori_loop(1, X * Z, send, 0)
        own = pltpu.make_async_copy(qn.at[z * X + x], qb.at[x, :, z], own_sem.at[2])
        own.start()
        return own

    def all_of(kind, p, sem):
        rows = QROWS - HROWS if kind == 2 else PART - (ROWS if p == 0 else 0)
        rest = kb.at[0, 0, 0, pl.ds(0, rows)]
        pltpu.make_async_copy(rest, rest, sem.at[kind, p]).wait()

    def near(t, i, p):
        block = bufs[t].at[c, y, p]
        return remote(block, block, near_send.at[t, i, p], near_recv.at[t, i, p], (dev_up, dev_down)[i])

    def far(t, i):
        block = bufs[t].at[c, (down, up)[i], i]
        return remote(block, block, far_send.at[t, i], far_recv.at[t, i], (dev_up, dev_down)[i])

    def swap(t, i, p):
        block = bufs[t].at[c, groups[i], p]
        return remote(block, block, swap_send.at[t, i, p], swap_recv.at[t, i, p], partner)

    def pass_own(t, p):
        if p == 0:
            own[t].wait()
        all_of(t, p, a2a_recv)
        near(t, 0, p).start()
        near(t, 1, p).start()
        swap(t, 0, p).start()

    def pass_near(t, p):
        for i in range(2):
            near(t, i, p).wait_recv()
            if i == p:
                far(t, i).start()
            swap(t, 1 + i, p).start()

    def pass_far(t):
        for i in range(2):
            far(t, i).wait_recv()
            swap(t, 3, i).start()

    own = [scatter_rows(0, lambda h: v_hbm.at[:, pl.ds(pl.multiple_of(h * HD, HD), HD)])]
    loads[0].wait()
    loads[1].wait()
    normalize_into(k_ref, gk_ref, kn)
    own.append(scatter_rows(1, lambda h: kn.at[h]))
    loads[2].wait()
    loads[3].wait()
    normalize_into(q_ref, gq_ref, qn)
    own.append(scatter_query())
    pass_own(0, 0)
    pass_own(0, 1)
    w_swap = remote(w_hbm, w_rows, w_sem.at[0], w_sem.at[1], partner)
    w_swap.start()
    for load in loads[4:6] + loads[7:]:
        load.wait()
    level = level_ref[lax.axis_index("frame")]
    hot = (lax.broadcasted_iota(jnp.int32, (8, gate_ref.shape[0]), 1) == level).astype(jnp.bfloat16)
    for sub in range(SUBS):
        where = pl.ds(sub * SUB, SUB)
        gate_row[:, where] = jnp.dot(hot, gate_ref[:, where], preferred_element_type=jnp.float32)[0:1]
        bias_row[:, where] = bias_ref[where].astype(jnp.float32)[None]
    pass_own(1, 0)
    pass_near(0, 0)
    pass_own(1, 1)
    pass_near(0, 1)

    def attend(hh, yy):
        query = qb[:, hh].reshape(QROWS, HD)
        keys = [kb[core, yy].reshape(GROUP, HD) for core in range(2)]
        values = [vb[core, yy].reshape(GROUP, HD) for core in range(2)]
        scores = [
            lax.dot_general(
                query, keys[core], (((1,), (1,)), ((), ())), preferred_element_type=jnp.float32
            )
            for core in range(2)
        ]
        key_stamp = [stamp_ref[yy * X + lax.rem(x + X - f, X)] for f in range(X)]
        summed = [None, None]
        weights = [[], []]
        alphas = []
        for g in range(X):
            stamp = stamp_ref[y * X + g]
            rows = slice(g * FROWS, (g + 1) * FROWS)
            best = jnp.full((FROWS, 128), 2 * HIDDEN, jnp.float32)
            shift = [jnp.where(key_stamp[f] <= stamp, 0.0, HIDDEN) for f in range(X)]
            for f in range(X):
                seen = None
                for core in range(2):
                    for i in (2 * f, 2 * f + 1):
                        tile = scores[core][rows, i * 128 : (i + 1) * 128]
                        seen = tile if seen is None else jnp.maximum(seen, tile)
                best = jnp.maximum(best, seen + shift[f])
            old = top_ref[hh, rows, :]
            new = jnp.maximum(old, jnp.max(best, axis=-1, keepdims=True) * SCALE)
            alpha = jnp.exp2(old - new)
            top_ref[hh, rows, :] = new
            total = sum_ref[hh, rows, :] * alpha
            column = new[:, 0:1]
            for core in range(2):
                row_weights = []
                for i in range(GROUP // 128):
                    piece = scores[core][rows, i * 128 : (i + 1) * 128]
                    exponent = jnp.exp2(piece * SCALE + (shift[i // 2] - column))
                    total = total + exponent
                    row_weights.append(exponent.astype(jnp.bfloat16))
                weights[core].append(jnp.concatenate(row_weights, axis=1))
            sum_ref[hh, rows, :] = total
            alphas.append(alpha)
        gained = sum(
            jnp.dot(
                jnp.concatenate(weights[core], axis=0), values[core], preferred_element_type=jnp.float32
            )
            for core in range(2)
        )
        acc_ref[hh] = acc_ref[hh] * jnp.concatenate(alphas, axis=0) + gained

    def cross(hh, d):
        tx = lax.rem(x + d, X)
        columns = pl.ds(pl.multiple_of(x * HD, HD), HD)
        return remote(
            att.at[hh, tx], a_ref.at[hh, :, columns], x_send.at[hh, d], x_recv.at[hh, d], device(tx, y, z, c)
        )

    def cross_own(hh):
        columns = pl.ds(pl.multiple_of(x * HD, HD), HD)
        return pltpu.make_async_copy(att.at[hh, x], a_ref.at[hh, :, columns], x_send.at[hh, 0])

    def finish(hh):
        total = jnp.sum(sum_ref[hh], axis=-1, keepdims=True)
        att[hh] = (acc_ref[hh] / total).astype(jnp.bfloat16).reshape(X, FROWS, HD)
        for d in range(1, X):
            cross(hh, d).start()
        cross_own(hh).start()

    def chunk(way, step):
        index = lax.rem(z + STEPS - step, Z) if way == 0 else lax.rem(z + STEPS + step, Z)
        return pl.ds(pl.multiple_of(index * HROWS, HROWS), HROWS)

    def opens(way, sub):
        return 0 if sub // (SUBS // 2) == way else 1

    def ring(hh, way, sub, step):
        where = pl.ds(sub * SUB, SUB)
        if step == opens(way, sub):
            source = part.at[hh, chunk(way, step), where]
        else:
            source = held.at[hh, way, step - 1, :, where]
        at = (hh, way, sub, step)
        return remote(
            source, held.at[hh, way, step, :, where], ring_send.at[at], ring_recv.at[at], (next_z, last_z)[way]
        )

    pairs = [(way, sub) for sub in range(SUBS // 2) for way, sub in ((0, sub), (1, sub + SUBS // 2))]
    pairs += [(1 - way, sub) for way, sub in pairs]

    def project(hh):
        for d in range(1, X):
            cross(hh, d).wait_recv()
        cross_own(hh).wait()
        for sub in range(SUBS):
            where = pl.ds(sub * SUB, SUB)
            part[hh, :, where] = jnp.dot(
                a_ref[hh], w_ref[:, where], preferred_element_type=jnp.float32
            ).astype(jnp.bfloat16)
            ring(hh, sub // (SUBS // 2), sub, 0).start()
        for sub in range(SUBS):
            ring(hh, 1 - sub // (SUBS // 2), sub, 1).start()

    def relay(hh, step):
        for way, sub in pairs:
            if step > opens(way, sub):
                ring(hh, way, sub, step - 1).wait_recv()
                where = pl.ds(sub * SUB, SUB)
                mine = part[hh, chunk(way, step), where].astype(jnp.float32)
                came = held[hh, way, step - 1, :, where].astype(jnp.float32)
                held[hh, way, step - 1, :, where] = (came + mine).astype(jnp.bfloat16)
                ring(hh, way, sub, step).start()

    def settle(hh):
        rows = pl.ds(hh * HROWS, HROWS)
        mine_rows = pl.ds(pl.multiple_of(z * HROWS, HROWS), HROWS)
        for sub in range(SUBS):
            where = pl.ds(sub * SUB, SUB)
            projected = part[hh, mine_rows, where].astype(jnp.float32)
            for way in range(2):
                ring(hh, way, sub, STEPS - 1).wait_recv()
                projected = projected + held[hh, way, STEPS - 1, :, where].astype(jnp.float32)
            mixed = tok_ref[rows, where].astype(jnp.float32) + gate_row[:, where] * (
                projected + bias_row[:, where]
            )
            out_ref[rows, where] = mixed.astype(jnp.bfloat16)

    top_ref[...] = jnp.full_like(top_ref, 2 * HIDDEN)
    sum_ref[...] = jnp.zeros_like(sum_ref)
    acc_ref[...] = jnp.zeros_like(acc_ref)
    own[2].wait()
    all_of(2, 0, a2a_recv)

    def wait_swap(i):
        for t in range(2):
            for p in range(PARTS):
                swap(t, i, p).wait_recv()

    order = ((0, 0), (1, 0), (0, 1), (0, 2), (0, 3), (1, 1), (1, 2), (1, 3))

    def choose(i, options):
        value = options[0]
        for n in range(1, len(options)):
            value = jnp.where(i == n, options[n], value)
        return value

    def step(i, carry):
        @pl.when(i == 0)
        def _():
            wait_swap(0)

        @pl.when(i == 1)
        def _():
            pass_near(1, 0)
            all_of(2, 1, a2a_recv)

        @pl.when(i == 2)
        def _():
            pass_near(1, 1)
            pass_far(0)
            wait_swap(1)

        @pl.when(i == 3)
        def _():
            wait_swap(2)
            pass_far(1)

        @pl.when(i == 4)
        def _():
            wait_swap(3)

        attend(choose(i, [hh for hh, _ in order]), choose(i, [groups[p] for _, p in order]))

        @pl.when(i == 4)
        def _():
            finish(0)

        @pl.when(i == 5)
        def _():
            loads[6].wait()
            w_swap.wait()
            project(0)

        @pl.when(i == 6)
        def _():
            relay(0, 1)

        return carry

    lax.fori_loop(0, len(order), step, 0)
    finish(1)
    relay(0, 2)
    project(1)
    relay(0, 3)
    relay(1, 1)
    settle(0)
    relay(1, 2)
    relay(1, 3)
    settle(1)

    for t in range(2):
        for i in range(2):
            for p in range(PARTS):
                near(t, i, p).wait_send()
            far(t, i).wait_send()
        for i in range(4):
            for p in range(PARTS):
                swap(t, i, p).wait_send()
    for kind in range(3):
        for p in range(PARTS):
            all_of(kind, p, a2a_send)
    for hh in range(HALVES):
        for d in range(1, X):
            cross(hh, d).wait_send()
        for way in range(2):
            for sub in range(SUBS):
                for s in range(opens(way, sub), STEPS):
                    ring(hh, way, sub, s).wait_send()


def shards(
    tokens, query_rows, key_rows, value_rows, gain_query, gain_key,
    out_weight, out_bias, gate_table, noise_level, slot_order,
):
    vmem = pl.BlockSpec(memory_space=pltpu.VMEM)
    hbm = pl.BlockSpec(memory_space=pltpu.HBM)
    bf16, f32 = jnp.bfloat16, jnp.float32
    dma = pltpu.SemaphoreType.DMA
    out = pl.pallas_call(
        fused_kernel,
        out_shape=jax.ShapeDtypeStruct((ROWS, D), bf16),
        in_specs=[hbm] * 11,
        out_specs=vmem,
        scratch_shapes=[
            pltpu.SMEM((X * Y,), jnp.int32),
            pltpu.SMEM((X * Y,), jnp.int32),
            pltpu.VMEM((ROWS, X * Z * HD), bf16),
            pltpu.VMEM((ROWS, X * Z * HD), bf16),
            pltpu.VMEM((1, X * Z * HD), f32),
            pltpu.VMEM((1, X * Z * HD), f32),
            pltpu.VMEM((X * Z, HALVES, HROWS, HD), bf16),
            pltpu.VMEM((X * Z, ROWS, HD), bf16),
            pltpu.VMEM((X, HALVES, Z, HROWS, HD), bf16),
            pltpu.VMEM((2, Y, PARTS, PART, HD), bf16),
            pltpu.VMEM((2, Y, PARTS, PART, HD), bf16),
            pltpu.VMEM((HALVES, QROWS, 128), f32),
            pltpu.VMEM((HALVES, QROWS, 128), f32),
            pltpu.VMEM((HALVES, QROWS, HD), f32),
            pltpu.VMEM((HALVES, X, FROWS, HD), bf16),
            pltpu.VMEM((HALVES, FROWS, DEPTH), bf16),
            pltpu.VMEM((DEPTH, D), bf16),
            pltpu.VMEM((HALVES, FROWS, D), bf16),
            pltpu.VMEM((HALVES, 2, STEPS, HROWS, D), bf16),
            pltpu.VMEM((ROWS, D), bf16),
            pltpu.VMEM((D,), bf16),
            pltpu.VMEM(gate_table.shape, bf16),
            pltpu.VMEM((1, D), f32),
            pltpu.VMEM((1, D), f32),
            dma((3, PARTS)), dma((3, PARTS)), dma((3,)),
            dma((2, 2, PARTS)), dma((2, 2, PARTS)), dma((2, 2)), dma((2, 2)), dma((2, 4, PARTS)), dma((2, 4, PARTS)),
            dma((2,)), dma((10,)), dma((HALVES, X)), dma((HALVES, X)),
            dma((HALVES, 2, SUBS, STEPS)), dma((HALVES, 2, SUBS, STEPS)),
        ],
        compiler_params=pltpu.CompilerParams(
            collective_id=0, has_side_effects=True, vmem_limit_bytes=48 * 2**20
        ),
        name="fused",
    )(
        *(
            pltpu.with_memory_space_constraint(array, pltpu.HBM)
            for array in (
                slot_order.astype(jnp.int32), noise_level.astype(jnp.int32),
                query_rows[0], key_rows[0], value_rows[0], gain_query[None], gain_key[None],
                out_weight, tokens[0], out_bias, gate_table,
            )
        )
    )
    return out[None]


def solution(mesh):
    placed = (
        P("frame", "seq", None), P("frame", "seq", None), P("frame", "seq", None), P("frame", "seq", None),
        P(), P(), P("seq", None), P(), P(), P(), P(),
    )
    return jax.shard_map(
        shards, mesh=mesh, in_specs=placed, out_specs=P("frame", "seq", None), check_vma=False
    )
```

```python
import functools

import jax
import jax.numpy as jnp
from jax import lax
from jax.experimental import pallas as pl
from jax.experimental.pallas import tpu as pltpu
from jax.sharding import PartitionSpec as P

HD = 128
EPS = 1e-06
X, Y, Z = 4, 4, 8
ROWS = 32
HALVES = 2
HROWS = ROWS // HALVES
QROWS = X * Z * HROWS
FROWS = Z * HROWS
GROUP = X * Z * ROWS
PARTS = X
PART = GROUP // PARTS
D = 5120
DEPTH = 512
SUBS = 2
SUB = D // SUBS
STEPS = Z // 2
MESH = pl.DeviceIdType.MESH
SCALE = HD ** -0.5 * 1.4426950408889634
HIDDEN = -1e30


def position():
    frame = lax.axis_index("frame")
    seq = lax.axis_index("seq")
    return lax.rem(frame, X), frame // X, seq // 2, lax.rem(seq, 2)


def device(x, y, z, c):
    return (y * X + x, z * 2 + c)


def remote(src, dst, send, recv, dev):
    return pltpu.make_async_remote_copy(
        src_ref=src, dst_ref=dst, send_sem=send, recv_sem=recv, device_id=dev, device_id_type=MESH
    )


def plane_peer(d, x, z):
    return lax.rem(x + lax.rem(d, X), X), lax.rem(z + d // X, Z)


def normalize_into(rows_ref, gain_ref, out_ref):
    values = rows_ref[...].astype(jnp.float32)
    inverse = lax.rsqrt(jnp.mean(values * values, axis=-1, keepdims=True) + EPS)
    for h in range(X * Z):
        at = slice(h * HD, (h + 1) * HD)
        part = (rows_ref[:, at].astype(jnp.float32) * inverse * gain_ref[:, at]).astype(jnp.bfloat16)
        out_ref[h] = part.reshape(out_ref.shape[1:])


def fused_kernel(
    stamp_hbm, level_hbm, q_hbm, k_hbm, v_hbm, gq_hbm, gk_hbm, w_hbm, tok_hbm, bias_hbm, gate_hbm,
    out_ref,
    stamp_ref, level_ref, q_ref, k_ref, gq_ref, gk_ref, qn, kn, qb, kb, vb, top_ref, sum_ref, acc_ref, att, a_ref, w_ref, part, held, tok_ref, bias_ref, gate_ref, bias_row, gate_row,
    a2a_send, a2a_recv, own_sem, ring_y_send, near_recv, far_recv, swap_send, swap_recv,
    w_sem, load_sem, x_send, x_own, x_recv, ring_send, ring_recv,
):
    x, y, z, c = position()
    up, down, opposite = lax.rem(y + 1, Y), lax.rem(y + Y - 1, Y), lax.rem(y + 2, Y)
    partner = device(x, y, z, 1 - c)
    dev_up, dev_down = device(x, up, z, c), device(x, down, z, c)
    next_z, last_z = device(x, y, lax.rem(z + 1, Z), c), device(x, y, lax.rem(z + Z - 1, Z), c)
    groups = (y, down, up, opposite)
    bufs = (vb, kb)

    barrier = pltpu.get_barrier_semaphore()

    def greet(i, carry):
        tx, tz = plane_peer(i + 1, x, z)
        pl.semaphore_signal(barrier, inc=1, device_id=device(tx, y, tz, c), device_id_type=MESH)
        return carry

    lax.fori_loop(0, X * Z - 1, greet, 0)
    for dev in (dev_up, dev_down, partner):
        pl.semaphore_signal(barrier, inc=1, device_id=dev, device_id_type=MESH)
    w_rows = w_ref.at[pl.ds(pl.multiple_of(c * (DEPTH // 2), DEPTH // 2), DEPTH // 2)]
    loads = [
        pltpu.make_async_copy(source, target, load_sem.at[i])
        for i, (source, target) in enumerate(
            (
                (k_hbm, k_ref), (gk_hbm, gk_ref), (q_hbm, q_ref), (gq_hbm, gq_ref),
                (stamp_hbm, stamp_ref), (level_hbm, level_ref), (w_hbm, w_rows), (tok_hbm, tok_ref), (bias_hbm, bias_ref), (gate_hbm, gate_ref),
            )
        )
    ]
    for load in loads:
        load.start()
    pl.semaphore_wait(barrier, X * Z - 1 + 3)

    def scatter(kind, p, first, source, target):
        def send(d, carry):
            dx, dz = first(d)
            tx, tz = lax.rem(x + dx, X), lax.rem(z + dz, Z)
            remote(
                source(tz * X + tx), target(dx), a2a_send.at[kind], a2a_recv.at[kind, p],
                device(tx, y, tz, c),
            ).start()
            return carry

        return send

    def farthest_first(k):
        return jnp.where(lax.rem(k, 2) == 1, (Z - 1 - k) // 2, lax.rem(Z // 2 + k // 2, Z))

    def scatter_rows(t, source):
        def target(dx):
            return bufs[t].at[c, y, dx, pl.ds(pl.multiple_of(z * ROWS, ROWS), ROWS)]

        for p in range(PARTS):
            send = scatter(t, p, lambda k: (p, farthest_first(k)), source, target)
            lax.fori_loop(0, Z - 1 if p == 0 else Z, send, 0)
        own = pltpu.make_async_copy(source(z * X + x), target(0), own_sem.at[t])
        own.start()
        return own

    def scatter_query():
        for hh in range(HALVES):
            send = scatter(
                2, hh, lambda d: (lax.rem(d + 1, X), farthest_first(d // X)),
                lambda h: qn.at[h, hh], lambda dx: qb.at[x, hh, z],
            )
            lax.fori_loop(0, X * Z - 1, send, 0)
        own = pltpu.make_async_copy(qn.at[z * X + x], qb.at[x, :, z], own_sem.at[2])
        own.start()
        return own

    def arrived(kind, p):
        if kind == 2:
            rest = qn.at[pl.ds(0, X * Z - 1), 0]
        else:
            rest = kb.at[0, 0, 0, pl.ds(0, PART - (ROWS if p == 0 else 0))]
        pltpu.make_async_copy(rest, rest, a2a_recv.at[kind, p]).wait()

    def near(t, i, p):
        block = bufs[t].at[c, y, p]
        return remote(block, block, ring_y_send, near_recv.at[t, i, p], (dev_up, dev_down)[i])

    def far(t, p):
        i = 2 * p // PARTS
        block = bufs[t].at[c, (down, up)[i], p]
        return remote(block, block, ring_y_send, far_recv.at[t, p], (dev_up, dev_down)[i])

    def swap(t, i, p):
        block = bufs[t].at[c, groups[i], p]
        return remote(block, block, swap_send, swap_recv.at[i], partner)

    def pass_own(t, p):
        if p == 0:
            own[t].wait()
        arrived(t, p)
        near(t, 0, p).start()
        near(t, 1, p).start()
        swap(t, 0, p).start()

    def pass_near(t, p):
        for i in range(2):
            near(t, i, p).wait_recv()
            if i == 2 * p // PARTS:
                far(t, p).start()
            swap(t, 1 + i, p).start()

    def pass_far(t):
        for p in (0, PARTS // 2, 1, PARTS // 2 + 1):
            far(t, p).wait_recv()
            swap(t, 3, p).start()

    def wait_swap(i):
        both = kb.at[:, 0]
        pltpu.make_async_copy(both, both, swap_recv.at[i]).wait()

    own = [scatter_rows(0, lambda h: v_hbm.at[:, pl.ds(pl.multiple_of(h * HD, HD), HD)])]
    w_swap = remote(w_hbm, w_rows, w_sem.at[0], w_sem.at[1], partner)
    w_swap.start()
    loads[0].wait()
    loads[1].wait()
    normalize_into(k_ref, gk_ref, kn)
    own.append(scatter_rows(1, lambda h: kn.at[h]))
    loads[2].wait()
    loads[3].wait()
    normalize_into(q_ref, gq_ref, qn)
    own.append(scatter_query())
    for p in range(PARTS):
        pass_own(0, p)
    for load in loads[4:6] + loads[7:]:
        load.wait()
    level = level_ref[lax.axis_index("frame")]
    hot = (lax.broadcasted_iota(jnp.int32, (8, gate_ref.shape[0]), 1) == level).astype(jnp.bfloat16)
    for sub in range(SUBS):
        where = pl.ds(sub * SUB, SUB)
        gate_row[:, where] = jnp.dot(hot, gate_ref[:, where], preferred_element_type=jnp.float32)[0:1]
        bias_row[:, where] = bias_ref[where].astype(jnp.float32)[None]
    for p in range(PARTS):
        pass_own(1, p)
    for p in range(PARTS):
        pass_near(0, p)

    def attend(hh, yy):
        query = qb[:, hh].reshape(QROWS, HD)
        keys = [kb[core, yy].reshape(GROUP, HD) for core in range(2)]
        values = [vb[core, yy].reshape(GROUP, HD) for core in range(2)]
        scores = [
            lax.dot_general(
                query, keys[core], (((1,), (1,)), ((), ())), preferred_element_type=jnp.float32
            )
            for core in range(2)
        ]
        key_stamp = [stamp_ref[yy * X + lax.rem(x + X - f, X)] for f in range(X)]
        summed = [None, None]
        weights = [[], []]
        alphas = []
        for g in range(X):
            stamp = stamp_ref[y * X + g]
            rows = slice(g * FROWS, (g + 1) * FROWS)
            best = jnp.full((FROWS, 128), 2 * HIDDEN, jnp.float32)
            shift = [jnp.where(key_stamp[f] <= stamp, 0.0, HIDDEN) for f in range(X)]
            for f in range(X):
                seen = None
                for core in range(2):
                    for i in (2 * f, 2 * f + 1):
                        tile = scores[core][rows, i * 128 : (i + 1) * 128]
                        seen = tile if seen is None else jnp.maximum(seen, tile)
                best = jnp.maximum(best, seen + shift[f])
            old = top_ref[hh, rows, :]
            new = jnp.maximum(old, jnp.max(best, axis=-1, keepdims=True) * SCALE)
            alpha = jnp.exp2(old - new)
            top_ref[hh, rows, :] = new
            total = sum_ref[hh, rows, :] * alpha
            column = new[:, 0:1]
            for core in range(2):
                row_weights = []
                for i in range(GROUP // 128):
                    piece = scores[core][rows, i * 128 : (i + 1) * 128]
                    exponent = jnp.exp2(piece * SCALE + (shift[i // 2] - column))
                    total = total + exponent
                    row_weights.append(exponent.astype(jnp.bfloat16))
                weights[core].append(jnp.concatenate(row_weights, axis=1))
            sum_ref[hh, rows, :] = total
            alphas.append(alpha)
        gained = sum(
            jnp.dot(
                jnp.concatenate(weights[core], axis=0), values[core], preferred_element_type=jnp.float32
            )
            for core in range(2)
        )
        acc_ref[hh] = acc_ref[hh] * jnp.concatenate(alphas, axis=0) + gained

    def cross(hh, d):
        tx = lax.rem(x + d, X)
        columns = pl.ds(pl.multiple_of(x * HD, HD), HD)
        return remote(
            att.at[hh, tx], a_ref.at[hh, :, columns], x_send, x_recv.at[hh], device(tx, y, z, c)
        )

    def cross_own(hh):
        columns = pl.ds(pl.multiple_of(x * HD, HD), HD)
        return pltpu.make_async_copy(att.at[hh, x], a_ref.at[hh, :, columns], x_own.at[hh])

    def finish(hh):
        total = jnp.sum(sum_ref[hh], axis=-1, keepdims=True)
        att[hh] = (acc_ref[hh] / total).astype(jnp.bfloat16).reshape(X, FROWS, HD)
        for d in range(1, X):
            cross(hh, d).start()
        cross_own(hh).start()

    def chunk(way, step):
        index = lax.rem(z + STEPS - step, Z) if way == 0 else lax.rem(z + STEPS + step, Z)
        return pl.ds(pl.multiple_of(index * HROWS, HROWS), HROWS)

    def opens(way, sub):
        return 0 if sub // (SUBS // 2) == way else 1

    def ring(hh, way, sub, step):
        where = pl.ds(sub * SUB, SUB)
        if step == opens(way, sub):
            source = part.at[hh, chunk(way, step), where]
        else:
            source = held.at[hh, way, step - 1, :, where]
        at = (hh, way, sub, step)
        return remote(
            source, held.at[hh, way, step, :, where], ring_send.at[hh], ring_recv.at[at], (next_z, last_z)[way]
        )

    pairs = [(way, sub) for sub in range(SUBS // 2) for way, sub in ((0, sub), (1, sub + SUBS // 2))]
    pairs += [(1 - way, sub) for way, sub in pairs]

    def project(hh):
        three = att.at[hh, pl.ds(0, X - 1)]
        pltpu.make_async_copy(three, three, x_recv.at[hh]).wait()
        cross_own(hh).wait()
        for sub in range(SUBS):
            where = pl.ds(sub * SUB, SUB)
            part[hh, :, where] = jnp.dot(
                a_ref[hh], w_ref[:, where], preferred_element_type=jnp.float32
            ).astype(jnp.bfloat16)
            ring(hh, sub // (SUBS // 2), sub, 0).start()
        for sub in range(SUBS):
            ring(hh, 1 - sub // (SUBS // 2), sub, 1).start()

    def relay(hh, step):
        for way, sub in pairs:
            if step > opens(way, sub):
                ring(hh, way, sub, step - 1).wait_recv()
                where = pl.ds(sub * SUB, SUB)
                mine = part[hh, chunk(way, step), where].astype(jnp.float32)
                came = held[hh, way, step - 1, :, where].astype(jnp.float32)
                held[hh, way, step - 1, :, where] = (came + mine).astype(jnp.bfloat16)
                ring(hh, way, sub, step).start()

    def settle(hh):
        rows = pl.ds(hh * HROWS, HROWS)
        mine_rows = pl.ds(pl.multiple_of(z * HROWS, HROWS), HROWS)
        for sub in range(SUBS):
            where = pl.ds(sub * SUB, SUB)
            projected = part[hh, mine_rows, where].astype(jnp.float32)
            for way in range(2):
                ring(hh, way, sub, STEPS - 1).wait_recv()
                projected = projected + held[hh, way, STEPS - 1, :, where].astype(jnp.float32)
            mixed = tok_ref[rows, where].astype(jnp.float32) + gate_row[:, where] * (
                projected + bias_row[:, where]
            )
            out_ref[rows, where] = mixed.astype(jnp.bfloat16)

    top_ref[...] = jnp.full_like(top_ref, 2 * HIDDEN)
    sum_ref[...] = jnp.zeros_like(sum_ref)
    acc_ref[...] = jnp.zeros_like(acc_ref)
    pass_near(1, 0)
    own[2].wait()
    arrived(2, 0)
    pass_near(1, 1)

    order = ((0, 0), (1, 0), (0, 1), (0, 2), (0, 3), (1, 1), (1, 2), (1, 3))

    def choose(i, options):
        value = options[0]
        for n in range(1, len(options)):
            value = jnp.where(i == n, options[n], value)
        return value

    def step(i, carry):
        @pl.when(i == 0)
        def _():
            wait_swap(0)

        @pl.when(i == 1)
        def _():
            pass_near(1, 2)
            pass_near(1, 3)
            arrived(2, 1)

        @pl.when(i == 2)
        def _():
            pass_far(0)
            wait_swap(1)

        @pl.when(i == 3)
        def _():
            wait_swap(2)
            pass_far(1)

        @pl.when(i == 4)
        def _():
            wait_swap(3)

        attend(choose(i, [hh for hh, _ in order]), choose(i, [groups[p] for _, p in order]))

        @pl.when(i == 4)
        def _():
            finish(0)

        @pl.when(i == 5)
        def _():
            loads[6].wait()
            w_swap.wait()
            project(0)

        @pl.when(i == 6)
        def _():
            relay(0, 1)

        return carry

    lax.fori_loop(0, len(order), step, 0)
    finish(1)
    relay(0, 2)
    project(1)
    relay(0, 3)
    relay(1, 1)
    settle(0)
    relay(1, 2)
    relay(1, 3)
    settle(1)

    def drain(ref, sem):
        pltpu.make_async_copy(ref, ref, sem).wait()

    for kind in range(3):
        drain(kn.at[pl.ds(0, X * Z - 1)], a2a_send.at[kind])
    drain(kb.at[:, pl.ds(0, 3)], ring_y_send)
    drain(kb, swap_send)
    drain(att.at[:, pl.ds(0, X - 1)], x_send)
    for hh in range(HALVES):
        drain(held.at[hh, :, :, :, pl.ds(0, D - D // (2 * STEPS))], ring_send.at[hh])


def shards(
    tokens, query_rows, key_rows, value_rows, gain_query, gain_key,
    out_weight, out_bias, gate_table, noise_level, slot_order,
):
    vmem = pl.BlockSpec(memory_space=pltpu.VMEM)
    hbm = pl.BlockSpec(memory_space=pltpu.HBM)
    bf16, f32 = jnp.bfloat16, jnp.float32
    dma = pltpu.SemaphoreType.DMA
    out = pl.pallas_call(
        fused_kernel,
        out_shape=jax.ShapeDtypeStruct((ROWS, D), bf16),
        in_specs=[hbm] * 11,
        out_specs=vmem,
        scratch_shapes=[
            pltpu.SMEM((X * Y,), jnp.int32),
            pltpu.SMEM((X * Y,), jnp.int32),
            pltpu.VMEM((ROWS, X * Z * HD), bf16),
            pltpu.VMEM((ROWS, X * Z * HD), bf16),
            pltpu.VMEM((1, X * Z * HD), f32),
            pltpu.VMEM((1, X * Z * HD), f32),
            pltpu.VMEM((X * Z, HALVES, HROWS, HD), bf16),
            pltpu.VMEM((X * Z, ROWS, HD), bf16),
            pltpu.VMEM((X, HALVES, Z, HROWS, HD), bf16),
            pltpu.VMEM((2, Y, PARTS, PART, HD), bf16),
            pltpu.VMEM((2, Y, PARTS, PART, HD), bf16),
            pltpu.VMEM((HALVES, QROWS, 128), f32),
            pltpu.VMEM((HALVES, QROWS, 128), f32),
            pltpu.VMEM((HALVES, QROWS, HD), f32),
            pltpu.VMEM((HALVES, X, FROWS, HD), bf16),
            pltpu.VMEM((HALVES, FROWS, DEPTH), bf16),
            pltpu.VMEM((DEPTH, D), bf16),
            pltpu.VMEM((HALVES, FROWS, D), bf16),
            pltpu.VMEM((HALVES, 2, STEPS, HROWS, D), bf16),
            pltpu.VMEM((ROWS, D), bf16),
            pltpu.VMEM((D,), bf16),
            pltpu.VMEM(gate_table.shape, bf16),
            pltpu.VMEM((1, D), f32),
            pltpu.VMEM((1, D), f32),
            dma((3,)), dma((3, PARTS)), dma((3,)), dma(()), dma((2, 2, PARTS)), dma((2, PARTS)), dma(()), dma((4,)),
            dma((2,)), dma((10,)), dma(()), dma((HALVES,)), dma((HALVES,)),
            dma((HALVES,)), dma((HALVES, 2, SUBS, STEPS)),
        ],
        compiler_params=pltpu.CompilerParams(
            collective_id=0, has_side_effects=True, vmem_limit_bytes=48 * 2**20
        ),
        name="fused",
    )(
        *(
            pltpu.with_memory_space_constraint(array, pltpu.HBM)
            for array in (
                slot_order.astype(jnp.int32), noise_level.astype(jnp.int32),
                query_rows[0], key_rows[0], value_rows[0], gain_query[None], gain_key[None],
                out_weight, tokens[0], out_bias, gate_table,
            )
        )
    )
    return out[None]


def solution(mesh):
    placed = (
        P("frame", "seq", None), P("frame", "seq", None), P("frame", "seq", None), P("frame", "seq", None),
        P(), P(), P("seq", None), P(), P(), P(), P(),
    )
    return jax.shard_map(
        shards, mesh=mesh, in_specs=placed, out_specs=P("frame", "seq", None), check_vma=False
    )
```

```python
import functools

import jax
import jax.numpy as jnp
from jax import lax
from jax.experimental import pallas as pl
from jax.experimental.pallas import tpu as pltpu
from jax.sharding import PartitionSpec as P

HD = 128
EPS = 1e-06
X, Y, Z = 4, 4, 8
ROWS = 32
HALVES = 2
HROWS = ROWS // HALVES
QROWS = X * Z * HROWS
FROWS = Z * HROWS
GROUP = X * Z * ROWS
PARTS = X
PART = GROUP // PARTS
D = 5120
DEPTH = 512
SUBS = 4
SUB = D // SUBS
STEPS = Z // 2
MESH = pl.DeviceIdType.MESH
SCALE = HD ** -0.5 * 1.4426950408889634
HIDDEN = -1e30


def position():
    frame = lax.axis_index("frame")
    seq = lax.axis_index("seq")
    return lax.rem(frame, X), frame // X, seq // 2, lax.rem(seq, 2)


def device(x, y, z, c):
    return (y * X + x, z * 2 + c)


def remote(src, dst, send, recv, dev):
    return pltpu.make_async_remote_copy(
        src_ref=src, dst_ref=dst, send_sem=send, recv_sem=recv, device_id=dev, device_id_type=MESH
    )


def normalize_into(rows_ref, gain_ref, out_ref):
    values = rows_ref[...].astype(jnp.float32)
    inverse = lax.rsqrt(jnp.mean(values * values, axis=-1, keepdims=True) + EPS)
    for h in range(X * Z):
        at = slice(h * HD, (h + 1) * HD)
        part = (rows_ref[:, at].astype(jnp.float32) * inverse * gain_ref[:, at]).astype(jnp.bfloat16)
        out_ref[h] = part.reshape(out_ref.shape[1:])


def fused_kernel(
    stamp_hbm, level_hbm, q_hbm, k_hbm, v_hbm, gq_hbm, gk_hbm, w_hbm, tok_hbm, bias_hbm, gate_hbm,
    out_ref,
    stamp_ref, level_ref, q_ref, k_ref, gq_ref, gk_ref, qn, kn, qb, kb, vb, top_ref, sum_ref, acc_ref, att, a_ref, w_ref, part, held, tok_ref, bias_ref, gate_ref, bias_row, gate_row,
    a2a_send, a2a_recv, own_sem, ring_y_send, near_recv, far_recv, swap_send, swap_recv,
    w_sem, load_sem, x_send, x_own, x_recv, ring_send, ring_recv,
):
    x, y, z, c = position()
    up, down, opposite = lax.rem(y + 1, Y), lax.rem(y + Y - 1, Y), lax.rem(y + 2, Y)
    partner = device(x, y, z, 1 - c)
    dev_up, dev_down = device(x, up, z, c), device(x, down, z, c)
    next_z, last_z = device(x, y, lax.rem(z + 1, Z), c), device(x, y, lax.rem(z + Z - 1, Z), c)
    groups = (y, down, up, opposite)
    bufs = (vb, kb)

    def farthest_first(k):
        return jnp.where(lax.rem(k, 2) == 1, (Z - 1 - k) // 2, lax.rem(Z // 2 + k // 2, Z))

    barrier = pltpu.get_barrier_semaphore()

    def greet(i, carry):
        tx, tz = lax.rem(x + i + 1, X), lax.rem(z + farthest_first(i // X), Z)
        pl.semaphore_signal(barrier, inc=1, device_id=device(tx, y, tz, c), device_id_type=MESH)
        return carry

    lax.fori_loop(0, X * Z - 1, greet, 0)
    for dev in (dev_up, dev_down, partner):
        pl.semaphore_signal(barrier, inc=1, device_id=dev, device_id_type=MESH)
    w_rows = w_ref.at[pl.ds(pl.multiple_of(c * (DEPTH // 2), DEPTH // 2), DEPTH // 2)]
    loads = [
        pltpu.make_async_copy(source, target, load_sem.at[i])
        for i, (source, target) in enumerate(
            (
                (k_hbm, k_ref), (gk_hbm, gk_ref), (q_hbm, q_ref), (gq_hbm, gq_ref),
                (stamp_hbm, stamp_ref), (level_hbm, level_ref), (w_hbm, w_rows), (tok_hbm, tok_ref), (bias_hbm, bias_ref), (gate_hbm, gate_ref),
            )
        )
    ]
    for load in loads:
        load.start()
    pl.semaphore_wait(barrier, X * Z - 1 + 3)

    def scatter(kind, p, first, source, target):
        def send(d, carry):
            dx, dz = first(d)
            tx, tz = lax.rem(x + dx, X), lax.rem(z + dz, Z)
            remote(
                source(tz * X + tx), target(dx), a2a_send.at[kind], a2a_recv.at[kind, p],
                device(tx, y, tz, c),
            ).start()
            return carry

        return send

    def scatter_rows(t, source):
        def target(dx):
            return bufs[t].at[c, y, dx, pl.ds(pl.multiple_of(z * ROWS, ROWS), ROWS)]

        for p in range(PARTS):
            send = scatter(t, p, lambda k: (p, farthest_first(k)), source, target)
            lax.fori_loop(0, Z - 1 if p == 0 else Z, send, 0)
        own = pltpu.make_async_copy(source(z * X + x), target(0), own_sem.at[t])
        own.start()
        return own

    def scatter_query():
        for hh in range(HALVES):
            send = scatter(
                2, hh, lambda d: (lax.rem(d + 1, X), farthest_first(d // X)),
                lambda h: qn.at[h, hh], lambda dx: qb.at[x, hh, z],
            )
            lax.fori_loop(0, X * Z - 1, send, 0)
        own = pltpu.make_async_copy(qn.at[z * X + x], qb.at[x, :, z], own_sem.at[2])
        own.start()
        return own

    def arrived(kind, p):
        if kind == 2:
            rest = qn.at[pl.ds(0, X * Z - 1), 0]
        else:
            rest = kb.at[0, 0, 0, pl.ds(0, PART - (ROWS if p == 0 else 0))]
        pltpu.make_async_copy(rest, rest, a2a_recv.at[kind, p]).wait()

    def near(t, i, p):
        block = bufs[t].at[c, y, p]
        return remote(block, block, ring_y_send, near_recv.at[t, i, p], (dev_up, dev_down)[i])

    def far(t, p):
        i = 2 * p // PARTS
        block = bufs[t].at[c, (down, up)[i], p]
        return remote(block, block, ring_y_send, far_recv.at[t, p], (dev_up, dev_down)[i])

    def swap(t, i, p):
        block = bufs[t].at[c, groups[i], p]
        return remote(block, block, swap_send, swap_recv.at[i], partner)

    def pass_own(t, p):
        if p == 0:
            own[t].wait()
        arrived(t, p)
        near(t, 0, p).start()
        near(t, 1, p).start()
        swap(t, 0, p).start()

    def pass_near(t, p):
        for i in range(2):
            near(t, i, p).wait_recv()
            if i == 2 * p // PARTS:
                far(t, p).start()
            swap(t, 1 + i, p).start()

    def pass_far(t):
        for p in (0, PARTS // 2, 1, PARTS // 2 + 1):
            far(t, p).wait_recv()
            swap(t, 3, p).start()

    def wait_swap(i):
        both = kb.at[:, 0]
        pltpu.make_async_copy(both, both, swap_recv.at[i]).wait()

    own = [scatter_rows(0, lambda h: v_hbm.at[:, pl.ds(pl.multiple_of(h * HD, HD), HD)])]
    w_swap = remote(w_hbm, w_rows, w_sem.at[0], w_sem.at[1], partner)
    w_swap.start()
    loads[0].wait()
    loads[1].wait()
    normalize_into(k_ref, gk_ref, kn)
    own.append(scatter_rows(1, lambda h: kn.at[h]))
    loads[2].wait()
    loads[3].wait()
    normalize_into(q_ref, gq_ref, qn)
    own.append(scatter_query())
    for p in range(PARTS):
        pass_own(0, p)
    for load in loads[4:6] + loads[7:]:
        load.wait()
    level = level_ref[lax.axis_index("frame")]
    hot = (lax.broadcasted_iota(jnp.int32, (8, gate_ref.shape[0]), 1) == level).astype(jnp.bfloat16)
    for sub in range(SUBS):
        where = pl.ds(sub * SUB, SUB)
        gate_row[:, where] = jnp.dot(hot, gate_ref[:, where], preferred_element_type=jnp.float32)[0:1]
        bias_row[:, where] = bias_ref[where].astype(jnp.float32)[None]
    for p in range(PARTS):
        pass_own(1, p)
    for p in range(PARTS):
        pass_near(0, p)

    def attend(hh, yy):
        query = qb[:, hh].reshape(QROWS, HD)
        keys = [kb[core, yy].reshape(GROUP, HD) for core in range(2)]
        values = [vb[core, yy].reshape(GROUP, HD) for core in range(2)]
        scores = [
            lax.dot_general(
                query, keys[core], (((1,), (1,)), ((), ())), preferred_element_type=jnp.float32
            )
            for core in range(2)
        ]
        key_stamp = [stamp_ref[yy * X + lax.rem(x + X - f, X)] for f in range(X)]
        summed = [None, None]
        weights = [[], []]
        alphas = []
        for g in range(X):
            stamp = stamp_ref[y * X + g]
            rows = slice(g * FROWS, (g + 1) * FROWS)
            best = jnp.full((FROWS, 128), 2 * HIDDEN, jnp.float32)
            shift = [jnp.where(key_stamp[f] <= stamp, 0.0, HIDDEN) for f in range(X)]
            for f in range(X):
                seen = None
                for core in range(2):
                    for i in (2 * f, 2 * f + 1):
                        tile = scores[core][rows, i * 128 : (i + 1) * 128]
                        seen = tile if seen is None else jnp.maximum(seen, tile)
                best = jnp.maximum(best, seen + shift[f])
            old = top_ref[hh, rows, :]
            new = jnp.maximum(old, jnp.max(best, axis=-1, keepdims=True) * SCALE)
            alpha = jnp.exp2(old - new)
            top_ref[hh, rows, :] = new
            total = sum_ref[hh, rows, :] * alpha
            column = new[:, 0:1]
            for core in range(2):
                row_weights = []
                for i in range(GROUP // 128):
                    piece = scores[core][rows, i * 128 : (i + 1) * 128]
                    exponent = jnp.exp2(piece * SCALE + (shift[i // 2] - column))
                    total = total + exponent
                    row_weights.append(exponent.astype(jnp.bfloat16))
                weights[core].append(jnp.concatenate(row_weights, axis=1))
            sum_ref[hh, rows, :] = total
            alphas.append(alpha)
        gained = sum(
            jnp.dot(
                jnp.concatenate(weights[core], axis=0), values[core], preferred_element_type=jnp.float32
            )
            for core in range(2)
        )
        acc_ref[hh] = acc_ref[hh] * jnp.concatenate(alphas, axis=0) + gained

    def cross(hh, d):
        tx = lax.rem(x + d, X)
        columns = pl.ds(pl.multiple_of(x * HD, HD), HD)
        return remote(
            att.at[hh, tx], a_ref.at[hh, :, columns], x_send, x_recv.at[hh], device(tx, y, z, c)
        )

    def cross_own(hh):
        columns = pl.ds(pl.multiple_of(x * HD, HD), HD)
        return pltpu.make_async_copy(att.at[hh, x], a_ref.at[hh, :, columns], x_own.at[hh])

    def finish(hh):
        total = jnp.sum(sum_ref[hh], axis=-1, keepdims=True)
        att[hh] = (acc_ref[hh] / total).astype(jnp.bfloat16).reshape(X, FROWS, HD)
        for d in range(1, X):
            cross(hh, d).start()
        cross_own(hh).start()

    def chunk(way, step):
        index = lax.rem(z + STEPS - step, Z) if way == 0 else lax.rem(z + STEPS + step, Z)
        return pl.ds(pl.multiple_of(index * HROWS, HROWS), HROWS)

    def opens(way, sub):
        return 0 if sub // (SUBS // 2) == way else 1

    def ring(hh, way, sub, step):
        where = pl.ds(sub * SUB, SUB)
        if step == opens(way, sub):
            source = part.at[hh, chunk(way, step), where]
        else:
            source = held.at[hh, way, step - 1, :, where]
        at = (hh, way, sub, step)
        return remote(
            source, held.at[hh, way, step, :, where], ring_send.at[hh], ring_recv.at[at], (next_z, last_z)[way]
        )

    pairs = [(way, sub) for sub in range(SUBS // 2) for way, sub in ((0, sub), (1, sub + SUBS // 2))]
    pairs += [(1 - way, sub) for way, sub in pairs]

    def project(hh):
        three = att.at[hh, pl.ds(0, X - 1)]
        pltpu.make_async_copy(three, three, x_recv.at[hh]).wait()
        cross_own(hh).wait()
        for way, sub in pairs[:SUBS]:
            where = pl.ds(sub * SUB, SUB)
            part[hh, :, where] = jnp.dot(
                a_ref[hh], w_ref[:, where], preferred_element_type=jnp.float32
            ).astype(jnp.bfloat16)
            ring(hh, way, sub, 0).start()
        for way, sub in pairs[SUBS:]:
            ring(hh, way, sub, 1).start()

    def relay(hh, step):
        for way, sub in pairs:
            if step > opens(way, sub):
                ring(hh, way, sub, step - 1).wait_recv()
                where = pl.ds(sub * SUB, SUB)
                mine = part[hh, chunk(way, step), where].astype(jnp.float32)
                came = held[hh, way, step - 1, :, where].astype(jnp.float32)
                held[hh, way, step - 1, :, where] = (came + mine).astype(jnp.bfloat16)
                ring(hh, way, sub, step).start()

    def settle(hh):
        rows = pl.ds(hh * HROWS, HROWS)
        mine_rows = pl.ds(pl.multiple_of(z * HROWS, HROWS), HROWS)
        for sub in range(SUBS):
            where = pl.ds(sub * SUB, SUB)
            projected = part[hh, mine_rows, where].astype(jnp.float32)
            for way in range(2):
                ring(hh, way, sub, STEPS - 1).wait_recv()
                projected = projected + held[hh, way, STEPS - 1, :, where].astype(jnp.float32)
            mixed = tok_ref[rows, where].astype(jnp.float32) + gate_row[:, where] * (
                projected + bias_row[:, where]
            )
            out_ref[rows, where] = mixed.astype(jnp.bfloat16)

    top_ref[...] = jnp.full_like(top_ref, 2 * HIDDEN)
    sum_ref[...] = jnp.zeros_like(sum_ref)
    acc_ref[...] = jnp.zeros_like(acc_ref)
    pass_near(1, 0)
    own[2].wait()
    arrived(2, 0)
    pass_near(1, 1)

    order = ((0, 0), (1, 0), (0, 1), (0, 2), (0, 3), (1, 1), (1, 2), (1, 3))

    def choose(i, options):
        value = options[0]
        for n in range(1, len(options)):
            value = jnp.where(i == n, options[n], value)
        return value

    def step(i, carry):
        @pl.when(i == 0)
        def _():
            wait_swap(0)

        @pl.when(i == 1)
        def _():
            pass_near(1, 2)
            pass_near(1, 3)
            arrived(2, 1)

        @pl.when(i == 2)
        def _():
            pass_far(0)
            wait_swap(1)

        @pl.when(i == 3)
        def _():
            wait_swap(2)
            pass_far(1)

        @pl.when(i == 4)
        def _():
            wait_swap(3)

        attend(choose(i, [hh for hh, _ in order]), choose(i, [groups[p] for _, p in order]))

        @pl.when(i == 4)
        def _():
            finish(0)

        @pl.when(i == 6)
        def _():
            loads[6].wait()
            w_swap.wait()
            project(0)

        return carry

    lax.fori_loop(0, len(order), step, 0)
    finish(1)
    relay(0, 1)
    project(1)
    relay(1, 1)
    relay(0, 2)
    relay(1, 2)
    relay(0, 3)
    relay(1, 3)
    settle(0)
    settle(1)

    def drain(ref, sem):
        pltpu.make_async_copy(ref, ref, sem).wait()

    for kind in range(3):
        drain(kn.at[pl.ds(0, X * Z - 1)], a2a_send.at[kind])
    drain(kb.at[:, pl.ds(0, 3)], ring_y_send)
    drain(kb, swap_send)
    drain(att.at[:, pl.ds(0, X - 1)], x_send)
    for hh in range(HALVES):
        drain(held.at[hh, :, :, :, pl.ds(0, D - D // (2 * STEPS))], ring_send.at[hh])


def shards(
    tokens, query_rows, key_rows, value_rows, gain_query, gain_key,
    out_weight, out_bias, gate_table, noise_level, slot_order,
):
    vmem = pl.BlockSpec(memory_space=pltpu.VMEM)
    hbm = pl.BlockSpec(memory_space=pltpu.HBM)
    bf16, f32 = jnp.bfloat16, jnp.float32
    dma = pltpu.SemaphoreType.DMA
    out = pl.pallas_call(
        fused_kernel,
        out_shape=jax.ShapeDtypeStruct((ROWS, D), bf16),
        in_specs=[hbm] * 11,
        out_specs=vmem,
        scratch_shapes=[
            pltpu.SMEM((X * Y,), jnp.int32),
            pltpu.SMEM((X * Y,), jnp.int32),
            pltpu.VMEM((ROWS, X * Z * HD), bf16),
            pltpu.VMEM((ROWS, X * Z * HD), bf16),
            pltpu.VMEM((1, X * Z * HD), f32),
            pltpu.VMEM((1, X * Z * HD), f32),
            pltpu.VMEM((X * Z, HALVES, HROWS, HD), bf16),
            pltpu.VMEM((X * Z, ROWS, HD), bf16),
            pltpu.VMEM((X, HALVES, Z, HROWS, HD), bf16),
            pltpu.VMEM((2, Y, PARTS, PART, HD), bf16),
            pltpu.VMEM((2, Y, PARTS, PART, HD), bf16),
            pltpu.VMEM((HALVES, QROWS, 128), f32),
            pltpu.VMEM((HALVES, QROWS, 128), f32),
            pltpu.VMEM((HALVES, QROWS, HD), f32),
            pltpu.VMEM((HALVES, X, FROWS, HD), bf16),
            pltpu.VMEM((HALVES, FROWS, DEPTH), bf16),
            pltpu.VMEM((DEPTH, D), bf16),
            pltpu.VMEM((HALVES, FROWS, D), bf16),
            pltpu.VMEM((HALVES, 2, STEPS, HROWS, D), bf16),
            pltpu.VMEM((ROWS, D), bf16),
            pltpu.VMEM((D,), bf16),
            pltpu.VMEM(gate_table.shape, bf16),
            pltpu.VMEM((1, D), f32),
            pltpu.VMEM((1, D), f32),
            dma((3,)), dma((3, PARTS)), dma((3,)), dma(()), dma((2, 2, PARTS)), dma((2, PARTS)), dma(()), dma((4,)),
            dma((2,)), dma((10,)), dma(()), dma((HALVES,)), dma((HALVES,)),
            dma((HALVES,)), dma((HALVES, 2, SUBS, STEPS)),
        ],
        compiler_params=pltpu.CompilerParams(
            collective_id=0, has_side_effects=True, vmem_limit_bytes=48 * 2**20
        ),
        name="fused",
    )(
        *(
            pltpu.with_memory_space_constraint(array, pltpu.HBM)
            for array in (
                slot_order.astype(jnp.int32), noise_level.astype(jnp.int32),
                query_rows[0], key_rows[0], value_rows[0], gain_query[None], gain_key[None],
                out_weight, tokens[0], out_bias, gate_table,
            )
        )
    )
    return out[None]


def solution(mesh):
    placed = (
        P("frame", "seq", None), P("frame", "seq", None), P("frame", "seq", None), P("frame", "seq", None),
        P(), P(), P("seq", None), P(), P(), P(), P(),
    )
    return jax.shard_map(
        shards, mesh=mesh, in_specs=placed, out_specs=P("frame", "seq", None), check_vma=False
    )
```

```python
import functools

import jax
import jax.numpy as jnp
from jax import lax
from jax.experimental import pallas as pl
from jax.experimental.pallas import tpu as pltpu
from jax.sharding import PartitionSpec as P

HD = 128
EPS = 1e-06
X, Y, Z = 4, 4, 8
ROWS = 32
HALVES = 2
HROWS = ROWS // HALVES
QROWS = X * Z * HROWS
FROWS = Z * HROWS
GROUP = X * Z * ROWS
PARTS = X
PART = GROUP // PARTS
D = 5120
DEPTH = 512
SUBS = 4
SUB = D // SUBS
STEPS = Z // 2
MESH = pl.DeviceIdType.MESH
SCALE = HD ** -0.5 * 1.4426950408889634
HIDDEN = -1e30


def position():
    frame = lax.axis_index("frame")
    seq = lax.axis_index("seq")
    return lax.rem(frame, X), frame // X, seq // 2, lax.rem(seq, 2)


def device(x, y, z, c):
    return (y * X + x, z * 2 + c)


def remote(src, dst, send, recv, dev):
    return pltpu.make_async_remote_copy(
        src_ref=src, dst_ref=dst, send_sem=send, recv_sem=recv, device_id=dev, device_id_type=MESH
    )


def normalize_into(rows_ref, gain_ref, out_ref):
    values = rows_ref[...].astype(jnp.float32)
    inverse = lax.rsqrt(jnp.mean(values * values, axis=-1, keepdims=True) + EPS)
    for h in range(X * Z):
        at = slice(h * HD, (h + 1) * HD)
        part = (rows_ref[:, at].astype(jnp.float32) * inverse * gain_ref[:, at]).astype(jnp.bfloat16)
        out_ref[h] = part.reshape(out_ref.shape[1:])


def fused_kernel(
    stamp_hbm, level_hbm, q_hbm, k_hbm, v_hbm, gq_hbm, gk_hbm, w_hbm, tok_hbm, bias_hbm, gate_hbm,
    out_ref,
    stamp_ref, level_ref, q_ref, k_ref, gq_ref, gk_ref, qn, kn, qb, kb, vb, top_ref, sum_ref, acc_ref, att, a_ref, w_ref, part, held, tok_ref, bias_ref, gate_ref, bias_row, gate_row,
    a2a_send, a2a_recv, own_sem, ring_y_send, near_recv, far_recv, swap_send, swap_recv,
    w_sem, load_sem, x_send, x_own, x_recv, ring_send, ring_recv,
):
    x, y, z, c = position()
    up, down, opposite = lax.rem(y + 1, Y), lax.rem(y + Y - 1, Y), lax.rem(y + 2, Y)
    partner = device(x, y, z, 1 - c)
    dev_up, dev_down = device(x, up, z, c), device(x, down, z, c)
    next_z, last_z = device(x, y, lax.rem(z + 1, Z), c), device(x, y, lax.rem(z + Z - 1, Z), c)
    groups = (y, down, up, opposite)
    bufs = (vb, kb)

    def farthest_first(k):
        if isinstance(k, int):
            return (Z - 1 - k) // 2 if k % 2 else (Z // 2 + k // 2) % Z
        return jnp.where(lax.rem(k, 2) == 1, (Z - 1 - k) // 2, lax.rem(Z // 2 + k // 2, Z))

    barrier = pltpu.get_barrier_semaphore()

    for dz in (4, 3, 5, 2, 6, 1, 7, 0):
        for dx in (2, 1, 3, 0):
            if dx or dz:
                peer = device(lax.rem(x + dx, X), y, lax.rem(z + dz, Z), c)
                pl.semaphore_signal(barrier, inc=1, device_id=peer, device_id_type=MESH)
    for dev in (dev_up, dev_down, partner):
        pl.semaphore_signal(barrier, inc=1, device_id=dev, device_id_type=MESH)
    w_rows = w_ref.at[pl.ds(pl.multiple_of(c * (DEPTH // 2), DEPTH // 2), DEPTH // 2)]
    loads = [
        pltpu.make_async_copy(source, target, load_sem.at[i])
        for i, (source, target) in enumerate(
            (
                (k_hbm, k_ref), (gk_hbm, gk_ref), (q_hbm, q_ref), (gq_hbm, gq_ref),
                (stamp_hbm, stamp_ref), (level_hbm, level_ref), (w_hbm, w_rows), (tok_hbm, tok_ref), (bias_hbm, bias_ref), (gate_hbm, gate_ref),
            )
        )
    ]
    for load in loads:
        load.start()
    pl.semaphore_wait(barrier, X * Z - 1 + 3)

    def scatter(kind, p, first, source, target):
        def send(d, carry):
            dx, dz = first(d)
            tx, tz = lax.rem(x + dx, X), lax.rem(z + dz, Z)
            remote(
                source(tz * X + tx), target(dx), a2a_send.at[kind], a2a_recv.at[kind, p],
                device(tx, y, tz, c),
            ).start()
            return carry

        return send

    def scatter_rows(t, source):
        def target(dx):
            return bufs[t].at[c, y, dx, pl.ds(pl.multiple_of(z * ROWS, ROWS), ROWS)]

        for p in range(PARTS):
            send = scatter(t, p, lambda k: (p, farthest_first(k)), source, target)
            for k in range(Z - 1 if p == 0 else Z):
                send(k, 0)
        own = pltpu.make_async_copy(source(z * X + x), target(0), own_sem.at[t])
        own.start()
        return own

    def scatter_query():
        for hh in range(HALVES):
            send = scatter(
                2, hh, lambda d: (lax.rem(d + 1, X), farthest_first(d // X)),
                lambda h: qn.at[h, hh], lambda dx: qb.at[x, hh, z],
            )
            lax.fori_loop(0, X * Z - 1, send, 0)
        own = pltpu.make_async_copy(qn.at[z * X + x], qb.at[x, :, z], own_sem.at[2])
        own.start()
        return own

    def arrived(kind, p):
        if kind == 2:
            rest = qn.at[pl.ds(0, X * Z - 1), 0]
        else:
            rest = kb.at[0, 0, 0, pl.ds(0, PART - (ROWS if p == 0 else 0))]
        pltpu.make_async_copy(rest, rest, a2a_recv.at[kind, p]).wait()

    def near(t, i, p):
        block = bufs[t].at[c, y, p]
        return remote(block, block, ring_y_send, near_recv.at[t, p], (dev_up, dev_down)[i])

    def far(t, p):
        i = 2 * p // PARTS
        block = bufs[t].at[c, (down, up)[i], p]
        return remote(block, block, ring_y_send, far_recv.at[t, p], (dev_up, dev_down)[i])

    def swap(t, i, p):
        block = bufs[t].at[c, groups[i], p]
        return remote(block, block, swap_send, swap_recv.at[i], partner)

    def pass_own(t, p):
        if p == 0:
            own[t].wait()
        arrived(t, p)
        near(t, 0, p).start()
        near(t, 1, p).start()
        swap(t, 0, p).start()

    def pass_near(t, p):
        pair = kb.at[0, 0, pl.ds(0, 2)]
        pltpu.make_async_copy(pair, pair, near_recv.at[t, p]).wait()
        far(t, p).start()
        swap(t, 1, p).start()
        swap(t, 2, p).start()

    def pass_far(t):
        for p in (0, PARTS // 2, 1, PARTS // 2 + 1):
            far(t, p).wait_recv()
            swap(t, 3, p).start()

    def wait_swap(i):
        both = kb.at[:, 0]
        pltpu.make_async_copy(both, both, swap_recv.at[i]).wait()

    own = [scatter_rows(0, lambda h: v_hbm.at[:, pl.ds(pl.multiple_of(h * HD, HD), HD)])]
    w_swap = remote(w_hbm, w_rows, w_sem.at[0], w_sem.at[1], partner)
    w_swap.start()
    loads[0].wait()
    loads[1].wait()
    normalize_into(k_ref, gk_ref, kn)
    own.append(scatter_rows(1, lambda h: kn.at[h]))
    loads[2].wait()
    loads[3].wait()
    normalize_into(q_ref, gq_ref, qn)
    own.append(scatter_query())
    for p in range(PARTS):
        pass_own(0, p)
    for load in loads[4:6] + loads[7:]:
        load.wait()
    level = level_ref[lax.axis_index("frame")]
    hot = (lax.broadcasted_iota(jnp.int32, (8, gate_ref.shape[0]), 1) == level).astype(jnp.bfloat16)
    for sub in range(SUBS):
        where = pl.ds(sub * SUB, SUB)
        gate_row[:, where] = jnp.dot(hot, gate_ref[:, where], preferred_element_type=jnp.float32)[0:1]
        bias_row[:, where] = bias_ref[where].astype(jnp.float32)[None]
    for p in range(PARTS):
        pass_own(1, p)
    for p in range(PARTS):
        pass_near(0, p)

    def attend(hh, groups_seen):
        query = qb[:, hh].reshape(QROWS, HD)
        pieces = [(yy, core) for yy in groups_seen for core in range(2)]
        scores = [
            lax.dot_general(
                query, kb[core, yy].reshape(GROUP, HD), (((1,), (1,)), ((), ())),
                preferred_element_type=jnp.float32,
            )
            for yy, core in pieces
        ]
        stamps = [[stamp_ref[yy * X + lax.rem(x + X - f, X)] for f in range(X)] for yy in groups_seen]
        weights = [[] for _ in pieces]
        alphas = []
        for g in range(X):
            stamp = stamp_ref[y * X + g]
            rows = slice(g * FROWS, (g + 1) * FROWS)
            best = jnp.full((FROWS, 128), 2 * HIDDEN, jnp.float32)
            shift = [[jnp.where(key <= stamp, 0.0, HIDDEN) for key in keys] for keys in stamps]
            for n in range(len(groups_seen)):
                for f in range(X):
                    seen = None
                    for score in scores[2 * n : 2 * n + 2]:
                        for i in (2 * f, 2 * f + 1):
                            tile = score[rows, i * 128 : (i + 1) * 128]
                            seen = tile if seen is None else jnp.maximum(seen, tile)
                    best = jnp.maximum(best, seen + shift[n][f])
            old = top_ref[hh, rows, :]
            new = jnp.maximum(old, jnp.max(best, axis=-1, keepdims=True) * SCALE)
            alpha = jnp.exp2(old - new)
            top_ref[hh, rows, :] = new
            total = sum_ref[hh, rows, :] * alpha
            column = new[:, 0:1]
            for m, score in enumerate(scores):
                row_weights = []
                for i in range(GROUP // 128):
                    piece = score[rows, i * 128 : (i + 1) * 128]
                    exponent = jnp.exp2(piece * SCALE + (shift[m // 2][i // 2] - column))
                    total = total + exponent
                    row_weights.append(exponent.astype(jnp.bfloat16))
                weights[m].append(jnp.concatenate(row_weights, axis=1))
            sum_ref[hh, rows, :] = total
            alphas.append(alpha)
        gained = sum(
            jnp.dot(
                jnp.concatenate(weights[m], axis=0), vb[core, yy].reshape(GROUP, HD),
                preferred_element_type=jnp.float32,
            )
            for m, (yy, core) in enumerate(pieces)
        )
        acc_ref[hh] = acc_ref[hh] * jnp.concatenate(alphas, axis=0) + gained

    def cross(hh, d):
        tx = lax.rem(x + d, X)
        columns = pl.ds(pl.multiple_of(x * HD, HD), HD)
        return remote(
            att.at[hh, tx], a_ref.at[hh, :, columns], x_send, x_recv.at[hh], device(tx, y, z, c)
        )

    def cross_own(hh):
        columns = pl.ds(pl.multiple_of(x * HD, HD), HD)
        return pltpu.make_async_copy(att.at[hh, x], a_ref.at[hh, :, columns], x_own.at[hh])

    def finish(hh):
        total = jnp.sum(sum_ref[hh], axis=-1, keepdims=True)
        att[hh] = (acc_ref[hh] / total).astype(jnp.bfloat16).reshape(X, FROWS, HD)
        for d in range(1, X):
            cross(hh, d).start()
        cross_own(hh).start()

    def chunk(way, step):
        index = lax.rem(z + STEPS - step, Z) if way == 0 else lax.rem(z + STEPS + step, Z)
        return pl.ds(pl.multiple_of(index * HROWS, HROWS), HROWS)

    def opens(way, sub):
        return 0 if sub // (SUBS // 2) == way else 1

    def ring(hh, way, sub, step):
        where = pl.ds(sub * SUB, SUB)
        if step == opens(way, sub):
            source = part.at[hh, chunk(way, step), where]
        else:
            source = held.at[hh, way, step - 1, :, where]
        at = (hh, way, sub, step)
        return remote(
            source, held.at[hh, way, step, :, where], ring_send.at[hh], ring_recv.at[at], (next_z, last_z)[way]
        )

    pairs = [(way, sub) for sub in range(SUBS // 2) for way, sub in ((0, sub), (1, sub + SUBS // 2))]
    pairs += [(1 - way, sub) for way, sub in pairs]

    def project(hh):
        three = att.at[hh, pl.ds(0, X - 1)]
        pltpu.make_async_copy(three, three, x_recv.at[hh]).wait()
        cross_own(hh).wait()
        for way, sub in pairs[:SUBS]:
            where = pl.ds(sub * SUB, SUB)
            part[hh, :, where] = jnp.dot(
                a_ref[hh], w_ref[:, where], preferred_element_type=jnp.float32
            ).astype(jnp.bfloat16)
            ring(hh, way, sub, 0).start()
        for way, sub in pairs[SUBS:]:
            ring(hh, way, sub, 1).start()

    def relay(hh, step):
        for way, sub in pairs:
            if step > opens(way, sub):
                ring(hh, way, sub, step - 1).wait_recv()
                where = pl.ds(sub * SUB, SUB)
                mine = part[hh, chunk(way, step), where].astype(jnp.float32)
                came = held[hh, way, step - 1, :, where].astype(jnp.float32)
                held[hh, way, step - 1, :, where] = (came + mine).astype(jnp.bfloat16)
                ring(hh, way, sub, step).start()

    def settle(hh):
        rows = pl.ds(hh * HROWS, HROWS)
        mine_rows = pl.ds(pl.multiple_of(z * HROWS, HROWS), HROWS)
        for sub in range(SUBS):
            where = pl.ds(sub * SUB, SUB)
            projected = part[hh, mine_rows, where].astype(jnp.float32)
            for way in range(2):
                ring(hh, way, sub, STEPS - 1).wait_recv()
                projected = projected + held[hh, way, STEPS - 1, :, where].astype(jnp.float32)
            mixed = tok_ref[rows, where].astype(jnp.float32) + gate_row[:, where] * (
                projected + bias_row[:, where]
            )
            out_ref[rows, where] = mixed.astype(jnp.bfloat16)

    top_ref[...] = jnp.full_like(top_ref, 2 * HIDDEN)
    sum_ref[...] = jnp.zeros_like(sum_ref)
    acc_ref[...] = jnp.zeros_like(acc_ref)
    pass_near(1, 0)
    own[2].wait()
    arrived(2, 0)
    pass_near(1, 1)

    order = ((0, 0), (1, 0), (0, 1), (0, 2), (0, 3))

    def choose(i, options):
        value = options[0]
        for n in range(1, len(options)):
            value = jnp.where(i == n, options[n], value)
        return value

    def step(i, carry):
        @pl.when(i == 0)
        def _():
            wait_swap(0)

        @pl.when(i == 1)
        def _():
            pass_near(1, 2)
            pass_near(1, 3)
            arrived(2, 1)

        @pl.when(i == 2)
        def _():
            pass_far(0)
            wait_swap(1)

        @pl.when(i == 3)
        def _():
            wait_swap(2)
            pass_far(1)

        @pl.when(i == 4)
        def _():
            wait_swap(3)

        attend(choose(i, [hh for hh, _ in order]), [choose(i, [groups[p] for _, p in order])])

        return carry

    lax.fori_loop(0, len(order), step, 0)
    finish(0)
    attend(1, (down, up, opposite))
    finish(1)
    loads[6].wait()
    w_swap.wait()
    project(0)
    project(1)
    relay(0, 1)
    relay(1, 1)
    relay(0, 2)
    relay(1, 2)
    relay(0, 3)
    relay(1, 3)
    settle(0)
    settle(1)

    def drain(ref, sem):
        pltpu.make_async_copy(ref, ref, sem).wait()

    for kind in range(3):
        drain(kn.at[pl.ds(0, X * Z - 1)], a2a_send.at[kind])
    drain(kb.at[:, pl.ds(0, 3)], ring_y_send)
    drain(kb, swap_send)
    drain(att.at[:, pl.ds(0, X - 1)], x_send)
    for hh in range(HALVES):
        drain(held.at[hh, :, :, :, pl.ds(0, D - D // (2 * STEPS))], ring_send.at[hh])


def shards(
    tokens, query_rows, key_rows, value_rows, gain_query, gain_key,
    out_weight, out_bias, gate_table, noise_level, slot_order,
):
    vmem = pl.BlockSpec(memory_space=pltpu.VMEM)
    hbm = pl.BlockSpec(memory_space=pltpu.HBM)
    bf16, f32 = jnp.bfloat16, jnp.float32
    dma = pltpu.SemaphoreType.DMA
    out = pl.pallas_call(
        fused_kernel,
        out_shape=jax.ShapeDtypeStruct((ROWS, D), bf16),
        in_specs=[hbm] * 11,
        out_specs=vmem,
        scratch_shapes=[
            pltpu.SMEM((X * Y,), jnp.int32),
            pltpu.SMEM((X * Y,), jnp.int32),
            pltpu.VMEM((ROWS, X * Z * HD), bf16),
            pltpu.VMEM((ROWS, X * Z * HD), bf16),
            pltpu.VMEM((1, X * Z * HD), f32),
            pltpu.VMEM((1, X * Z * HD), f32),
            pltpu.VMEM((X * Z, HALVES, HROWS, HD), bf16),
            pltpu.VMEM((X * Z, ROWS, HD), bf16),
            pltpu.VMEM((X, HALVES, Z, HROWS, HD), bf16),
            pltpu.VMEM((2, Y, PARTS, PART, HD), bf16),
            pltpu.VMEM((2, Y, PARTS, PART, HD), bf16),
            pltpu.VMEM((HALVES, QROWS, 128), f32),
            pltpu.VMEM((HALVES, QROWS, 128), f32),
            pltpu.VMEM((HALVES, QROWS, HD), f32),
            pltpu.VMEM((HALVES, X, FROWS, HD), bf16),
            pltpu.VMEM((HALVES, FROWS, DEPTH), bf16),
            pltpu.VMEM((DEPTH, D), bf16),
            pltpu.VMEM((HALVES, FROWS, D), bf16),
            pltpu.VMEM((HALVES, 2, STEPS, HROWS, D), bf16),
            pltpu.VMEM((ROWS, D), bf16),
            pltpu.VMEM((D,), bf16),
            pltpu.VMEM(gate_table.shape, bf16),
            pltpu.VMEM((1, D), f32),
            pltpu.VMEM((1, D), f32),
            dma((3,)), dma((3, PARTS)), dma((3,)), dma(()), dma((2, PARTS)), dma((2, PARTS)), dma(()), dma((4,)),
            dma((2,)), dma((10,)), dma(()), dma((HALVES,)), dma((HALVES,)),
            dma((HALVES,)), dma((HALVES, 2, SUBS, STEPS)),
        ],
        compiler_params=pltpu.CompilerParams(
            collective_id=0, has_side_effects=True, vmem_limit_bytes=48 * 2**20
        ),
        name="fused",
    )(
        *(
            pltpu.with_memory_space_constraint(array, pltpu.HBM)
            for array in (
                slot_order.astype(jnp.int32), noise_level.astype(jnp.int32),
                query_rows[0], key_rows[0], value_rows[0], gain_query[None], gain_key[None],
                out_weight, tokens[0], out_bias, gate_table,
            )
        )
    )
    return out[None]


def solution(mesh):
    placed = (
        P("frame", "seq", None), P("frame", "seq", None), P("frame", "seq", None), P("frame", "seq", None),
        P(), P(), P("seq", None), P(), P(), P(), P(),
    )
    return jax.shard_map(
        shards, mesh=mesh, in_specs=placed, out_specs=P("frame", "seq", None), check_vma=False
    )
```

```python
import functools

import jax
import jax.numpy as jnp
from jax import lax
from jax.experimental import pallas as pl
from jax.experimental.pallas import tpu as pltpu
from jax.sharding import PartitionSpec as P

HD = 128
EPS = 1e-06
X, Y, Z = 4, 4, 8
ROWS = 32
HALVES = 2
HROWS = ROWS // HALVES
QROWS = X * Z * HROWS
FROWS = Z * HROWS
GROUP = X * Z * ROWS
PARTS = X
PART = GROUP // PARTS
D = 5120
DEPTH = 512
SUBS = 4
SUB = D // SUBS
STEPS = Z // 2
MESH = pl.DeviceIdType.MESH
SCALE = HD ** -0.5 * 1.4426950408889634
HIDDEN = -1e30


def position():
    frame = lax.axis_index("frame")
    seq = lax.axis_index("seq")
    return lax.rem(frame, X), frame // X, seq // 2, lax.rem(seq, 2)


def device(x, y, z, c):
    return (y * X + x, z * 2 + c)


def remote(src, dst, send, recv, dev):
    return pltpu.make_async_remote_copy(
        src_ref=src, dst_ref=dst, send_sem=send, recv_sem=recv, device_id=dev, device_id_type=MESH
    )


def normalize_into(rows_ref, gain_ref, out_ref):
    values = rows_ref[...].astype(jnp.float32)
    inverse = lax.rsqrt(jnp.mean(values * values, axis=-1, keepdims=True) + EPS)
    for h in range(X * Z):
        at = slice(h * HD, (h + 1) * HD)
        part = (rows_ref[:, at].astype(jnp.float32) * inverse * gain_ref[:, at]).astype(jnp.bfloat16)
        out_ref[h] = part.reshape(out_ref.shape[1:])


def fused_kernel(
    stamp_hbm, level_hbm, q_hbm, k_hbm, v_hbm, gq_hbm, gk_hbm, w_hbm, tok_hbm, bias_hbm, gate_hbm,
    out_ref,
    stamp_ref, level_ref, q_ref, k_ref, gq_ref, gk_ref, qn, kn, qb, kb, vb, top_ref, sum_ref, acc_ref, att, a_ref, w_ref, part, held, tok_ref, bias_ref, gate_ref, bias_row, gate_row,
    a2a_send, a2a_recv, own_sem, ring_y_send, near_recv, far_recv, swap_send, swap_recv,
    w_sem, load_sem, x_send, x_own, x_recv, ring_send, ring_recv,
):
    x, y, z, c = position()
    up, down, opposite = lax.rem(y + 1, Y), lax.rem(y + Y - 1, Y), lax.rem(y + 2, Y)
    partner = device(x, y, z, 1 - c)
    dev_up, dev_down = device(x, up, z, c), device(x, down, z, c)
    next_z, last_z = device(x, y, lax.rem(z + 1, Z), c), device(x, y, lax.rem(z + Z - 1, Z), c)
    groups = (y, down, up, opposite)
    bufs = (vb, kb)

    def farthest_first(k):
        if isinstance(k, int):
            return (Z - 1 - k) // 2 if k % 2 else (Z // 2 + k // 2) % Z
        return jnp.where(lax.rem(k, 2) == 1, (Z - 1 - k) // 2, lax.rem(Z // 2 + k // 2, Z))

    barrier = pltpu.get_barrier_semaphore()

    for dz in (4, 3, 5, 2, 6, 1, 7, 0):
        for dx in (2, 1, 3, 0):
            if dx or dz:
                peer = device(lax.rem(x + dx, X), y, lax.rem(z + dz, Z), c)
                pl.semaphore_signal(barrier, inc=1, device_id=peer, device_id_type=MESH)
    for dev in (dev_up, dev_down, partner):
        pl.semaphore_signal(barrier, inc=1, device_id=dev, device_id_type=MESH)
    w_rows = w_ref.at[pl.ds(pl.multiple_of(c * (DEPTH // 2), DEPTH // 2), DEPTH // 2)]
    loads = [
        pltpu.make_async_copy(source, target, load_sem.at[i])
        for i, (source, target) in enumerate(
            (
                (k_hbm, k_ref), (gk_hbm, gk_ref), (q_hbm, q_ref), (gq_hbm, gq_ref),
                (stamp_hbm, stamp_ref), (level_hbm, level_ref), (w_hbm, w_rows), (tok_hbm, tok_ref), (bias_hbm, bias_ref), (gate_hbm, gate_ref),
            )
        )
    ]
    for load in loads:
        load.start()
    pl.semaphore_wait(barrier, X * Z - 1 + 3)

    def scatter(kind, p, first, source, target):
        def send(d, carry):
            dx, dz = first(d)
            tx, tz = lax.rem(x + dx, X), lax.rem(z + dz, Z)
            remote(
                source(tz * X + tx), target(dx), a2a_send.at[kind], a2a_recv.at[kind, p],
                device(tx, y, tz, c),
            ).start()
            return carry

        return send

    def scatter_rows(t, source):
        def target(dx):
            return bufs[t].at[c, y, dx, pl.ds(pl.multiple_of(z * ROWS, ROWS), ROWS)]

        for p in range(PARTS):
            send = scatter(t, p, lambda k: (p, farthest_first(k)), source, target)
            for k in range(Z - 1 if p == 0 else Z):
                send(k, 0)
        own = pltpu.make_async_copy(source(z * X + x), target(0), own_sem.at[t])
        own.start()
        return own

    def scatter_query():
        for hh in range(HALVES):
            send = scatter(
                2, hh, lambda d: (lax.rem(d + 1, X), farthest_first(d // X)),
                lambda h: qn.at[h, hh], lambda dx: qb.at[x, hh, z],
            )
            lax.fori_loop(0, X * Z - 1, send, 0)
        own = pltpu.make_async_copy(qn.at[z * X + x], qb.at[x, :, z], own_sem.at[2])
        own.start()
        return own

    def arrived(kind, p):
        if kind == 2:
            rest = qn.at[pl.ds(0, X * Z - 1), 0]
        else:
            rest = kb.at[0, 0, 0, pl.ds(0, PART - (ROWS if p == 0 else 0))]
        pltpu.make_async_copy(rest, rest, a2a_recv.at[kind, p]).wait()

    def near(t, i, p):
        block = bufs[t].at[c, y, p]
        return remote(block, block, ring_y_send, near_recv.at[t, p], (dev_up, dev_down)[i])

    def far(t, p):
        i = 2 * p // PARTS
        block = bufs[t].at[c, (down, up)[i], p]
        return remote(block, block, ring_y_send, far_recv.at[t, p], (dev_up, dev_down)[i])

    def swap(t, i, p):
        block = bufs[t].at[c, groups[i], p]
        return remote(block, block, swap_send, swap_recv.at[i], partner)

    def pass_own(t, p):
        if p == 0:
            own[t].wait()
        arrived(t, p)
        near(t, 0, p).start()
        near(t, 1, p).start()
        swap(t, 0, p).start()

    def pass_near(t, p):
        pair = kb.at[0, 0, pl.ds(0, 2)]
        pltpu.make_async_copy(pair, pair, near_recv.at[t, p]).wait()
        far(t, p).start()
        swap(t, 1, p).start()
        swap(t, 2, p).start()

    def pass_far(t):
        for p in (0, PARTS // 2, 1, PARTS // 2 + 1):
            far(t, p).wait_recv()
            swap(t, 3, p).start()

    def wait_swap(i):
        both = kb.at[:, 0]
        pltpu.make_async_copy(both, both, swap_recv.at[i]).wait()

    own = [scatter_rows(0, lambda h: v_hbm.at[:, pl.ds(pl.multiple_of(h * HD, HD), HD)])]
    w_swap = remote(w_hbm, w_rows, w_sem.at[0], w_sem.at[1], partner)
    w_swap.start()
    loads[0].wait()
    loads[1].wait()
    normalize_into(k_ref, gk_ref, kn)
    own.append(scatter_rows(1, lambda h: kn.at[h]))
    loads[2].wait()
    loads[3].wait()
    normalize_into(q_ref, gq_ref, qn)
    own.append(scatter_query())
    for p in range(PARTS):
        pass_own(0, p)
    for load in loads[4:6] + loads[7:]:
        load.wait()
    level = level_ref[lax.axis_index("frame")]
    hot = (lax.broadcasted_iota(jnp.int32, (8, gate_ref.shape[0]), 1) == level).astype(jnp.bfloat16)
    for sub in range(SUBS):
        where = pl.ds(sub * SUB, SUB)
        gate_row[:, where] = jnp.dot(hot, gate_ref[:, where], preferred_element_type=jnp.float32)[0:1]
        bias_row[:, where] = bias_ref[where].astype(jnp.float32)[None]
    for p in range(PARTS):
        pass_own(1, p)
    for p in range(PARTS):
        pass_near(0, p)

    def attend(hh, groups_seen):
        query = qb[:, hh].reshape(QROWS, HD)
        pieces = [(yy, core) for yy in groups_seen for core in range(2)]
        scores = [
            lax.dot_general(
                query, kb[core, yy].reshape(GROUP, HD), (((1,), (1,)), ((), ())),
                preferred_element_type=jnp.float32,
            )
            for yy, core in pieces
        ]
        stamps = [[stamp_ref[yy * X + lax.rem(x + X - f, X)] for f in range(X)] for yy in groups_seen]
        weights = [[] for _ in pieces]
        alphas = []
        for g in range(X):
            stamp = stamp_ref[y * X + g]
            rows = slice(g * FROWS, (g + 1) * FROWS)
            best = jnp.full((FROWS, 128), 2 * HIDDEN, jnp.float32)
            shift = [[jnp.where(key <= stamp, 0.0, HIDDEN) for key in keys] for keys in stamps]
            for n in range(len(groups_seen)):
                for f in range(X):
                    seen = None
                    for score in scores[2 * n : 2 * n + 2]:
                        for i in (2 * f, 2 * f + 1):
                            tile = score[rows, i * 128 : (i + 1) * 128]
                            seen = tile if seen is None else jnp.maximum(seen, tile)
                    best = jnp.maximum(best, seen + shift[n][f])
            old = top_ref[hh, rows, :]
            new = jnp.maximum(old, jnp.max(best, axis=-1, keepdims=True) * SCALE)
            alpha = jnp.exp2(old - new)
            top_ref[hh, rows, :] = new
            total = sum_ref[hh, rows, :] * alpha
            column = new[:, 0:1]
            for m, score in enumerate(scores):
                row_weights = []
                for i in range(GROUP // 128):
                    piece = score[rows, i * 128 : (i + 1) * 128]
                    exponent = jnp.exp2(piece * SCALE + (shift[m // 2][i // 2] - column))
                    total = total + exponent
                    row_weights.append(exponent.astype(jnp.bfloat16))
                weights[m].append(jnp.concatenate(row_weights, axis=1))
            sum_ref[hh, rows, :] = total
            alphas.append(alpha)
        gained = sum(
            jnp.dot(
                jnp.concatenate(weights[m], axis=0), vb[core, yy].reshape(GROUP, HD),
                preferred_element_type=jnp.float32,
            )
            for m, (yy, core) in enumerate(pieces)
        )
        acc_ref[hh] = acc_ref[hh] * jnp.concatenate(alphas, axis=0) + gained

    def cross(hh, d):
        tx = lax.rem(x + d, X)
        columns = pl.ds(pl.multiple_of(x * HD, HD), HD)
        return remote(
            att.at[hh, tx], a_ref.at[hh, :, columns], x_send, x_recv.at[hh], device(tx, y, z, c)
        )

    def cross_own(hh):
        columns = pl.ds(pl.multiple_of(x * HD, HD), HD)
        return pltpu.make_async_copy(att.at[hh, x], a_ref.at[hh, :, columns], x_own.at[hh])

    def finish(hh):
        total = jnp.sum(sum_ref[hh], axis=-1, keepdims=True)
        att[hh] = (acc_ref[hh] / total).astype(jnp.bfloat16).reshape(X, FROWS, HD)
        for d in range(1, X):
            cross(hh, d).start()
        cross_own(hh).start()

    def chunk(way, step):
        index = lax.rem(z + STEPS - step, Z) if way == 0 else lax.rem(z + STEPS + step, Z)
        return pl.ds(pl.multiple_of(index * HROWS, HROWS), HROWS)

    def opens(way, sub):
        return 0 if sub // (SUBS // 2) == way else 1

    def ring(hh, way, sub, step):
        where = pl.ds(sub * SUB, SUB)
        if step == opens(way, sub):
            source = part.at[hh, chunk(way, step), where]
        else:
            source = held.at[hh, way, step - 1, :, where]
        at = (hh, way, sub, step)
        return remote(
            source, held.at[hh, way, step, :, where], ring_send.at[hh], ring_recv.at[at], (next_z, last_z)[way]
        )

    pairs = [(way, sub) for sub in range(SUBS // 2) for way, sub in ((0, sub), (1, sub + SUBS // 2))]
    pairs += [(1 - way, sub) for way, sub in pairs]

    def project(hh):
        three = att.at[hh, pl.ds(0, X - 1)]
        pltpu.make_async_copy(three, three, x_recv.at[hh]).wait()
        cross_own(hh).wait()
        for way, sub in pairs[:SUBS]:
            where = pl.ds(sub * SUB, SUB)
            part[hh, :, where] = jnp.dot(
                a_ref[hh], w_ref[:, where], preferred_element_type=jnp.float32
            ).astype(jnp.bfloat16)
            ring(hh, way, sub, 0).start()
        for way, sub in pairs[SUBS:]:
            ring(hh, way, sub, 1).start()

    def relay(hh, step):
        for way, sub in pairs:
            if step > opens(way, sub):
                ring(hh, way, sub, step - 1).wait_recv()
                where = pl.ds(sub * SUB, SUB)
                mine = part[hh, chunk(way, step), where].astype(jnp.float32)
                came = held[hh, way, step - 1, :, where].astype(jnp.float32)
                held[hh, way, step - 1, :, where] = (came + mine).astype(jnp.bfloat16)
                ring(hh, way, sub, step).start()

    def settle(hh):
        rows = pl.ds(hh * HROWS, HROWS)
        mine_rows = pl.ds(pl.multiple_of(z * HROWS, HROWS), HROWS)
        for sub in range(SUBS):
            where = pl.ds(sub * SUB, SUB)
            projected = part[hh, mine_rows, where].astype(jnp.float32)
            for way in range(2):
                ring(hh, way, sub, STEPS - 1).wait_recv()
                projected = projected + held[hh, way, STEPS - 1, :, where].astype(jnp.float32)
            mixed = tok_ref[rows, where].astype(jnp.float32) + gate_row[:, where] * (
                projected + bias_row[:, where]
            )
            out_ref[rows, where] = mixed.astype(jnp.bfloat16)

    top_ref[...] = jnp.full_like(top_ref, 2 * HIDDEN)
    sum_ref[...] = jnp.zeros_like(sum_ref)
    acc_ref[...] = jnp.zeros_like(acc_ref)
    pass_near(1, 0)
    own[2].wait()
    arrived(2, 0)
    pass_near(1, 1)

    wait_swap(0)

    def opening(hh, carry):
        @pl.when(hh == 1)
        def _():
            pass_near(1, 2)
            pass_near(1, 3)
            arrived(2, 1)

        attend(hh, (y,))
        return carry

    lax.fori_loop(0, HALVES, opening, 0)
    pass_far(0)
    wait_swap(1)
    wait_swap(2)
    pass_far(1)
    attend(0, (down, up))
    wait_swap(3)
    attend(0, (opposite,))
    finish(0)
    attend(1, (down, up, opposite))
    finish(1)
    loads[6].wait()
    w_swap.wait()
    project(0)
    project(1)
    relay(0, 1)
    relay(1, 1)
    relay(0, 2)
    relay(1, 2)
    relay(0, 3)
    relay(1, 3)
    settle(0)
    settle(1)

    def drain(ref, sem):
        pltpu.make_async_copy(ref, ref, sem).wait()

    for kind in range(3):
        drain(kn.at[pl.ds(0, X * Z - 1)], a2a_send.at[kind])
    drain(kb.at[:, pl.ds(0, 3)], ring_y_send)
    drain(kb, swap_send)
    drain(att.at[:, pl.ds(0, X - 1)], x_send)
    for hh in range(HALVES):
        drain(held.at[hh, :, :, :, pl.ds(0, D - D // (2 * STEPS))], ring_send.at[hh])


def shards(
    tokens, query_rows, key_rows, value_rows, gain_query, gain_key,
    out_weight, out_bias, gate_table, noise_level, slot_order,
):
    vmem = pl.BlockSpec(memory_space=pltpu.VMEM)
    hbm = pl.BlockSpec(memory_space=pltpu.HBM)
    bf16, f32 = jnp.bfloat16, jnp.float32
    dma = pltpu.SemaphoreType.DMA
    out = pl.pallas_call(
        fused_kernel,
        out_shape=jax.ShapeDtypeStruct((ROWS, D), bf16),
        in_specs=[hbm] * 11,
        out_specs=vmem,
        scratch_shapes=[
            pltpu.SMEM((X * Y,), jnp.int32),
            pltpu.SMEM((X * Y,), jnp.int32),
            pltpu.VMEM((ROWS, X * Z * HD), bf16),
            pltpu.VMEM((ROWS, X * Z * HD), bf16),
            pltpu.VMEM((1, X * Z * HD), f32),
            pltpu.VMEM((1, X * Z * HD), f32),
            pltpu.VMEM((X * Z, HALVES, HROWS, HD), bf16),
            pltpu.VMEM((X * Z, ROWS, HD), bf16),
            pltpu.VMEM((X, HALVES, Z, HROWS, HD), bf16),
            pltpu.VMEM((2, Y, PARTS, PART, HD), bf16),
            pltpu.VMEM((2, Y, PARTS, PART, HD), bf16),
            pltpu.VMEM((HALVES, QROWS, 128), f32),
            pltpu.VMEM((HALVES, QROWS, 128), f32),
            pltpu.VMEM((HALVES, QROWS, HD), f32),
            pltpu.VMEM((HALVES, X, FROWS, HD), bf16),
            pltpu.VMEM((HALVES, FROWS, DEPTH), bf16),
            pltpu.VMEM((DEPTH, D), bf16),
            pltpu.VMEM((HALVES, FROWS, D), bf16),
            pltpu.VMEM((HALVES, 2, STEPS, HROWS, D), bf16),
            pltpu.VMEM((ROWS, D), bf16),
            pltpu.VMEM((D,), bf16),
            pltpu.VMEM(gate_table.shape, bf16),
            pltpu.VMEM((1, D), f32),
            pltpu.VMEM((1, D), f32),
            dma((3,)), dma((3, PARTS)), dma((3,)), dma(()), dma((2, PARTS)), dma((2, PARTS)), dma(()), dma((4,)),
            dma((2,)), dma((10,)), dma(()), dma((HALVES,)), dma((HALVES,)),
            dma((HALVES,)), dma((HALVES, 2, SUBS, STEPS)),
        ],
        compiler_params=pltpu.CompilerParams(
            collective_id=0, has_side_effects=True, vmem_limit_bytes=48 * 2**20
        ),
        name="fused",
    )(
        *(
            pltpu.with_memory_space_constraint(array, pltpu.HBM)
            for array in (
                slot_order.astype(jnp.int32), noise_level.astype(jnp.int32),
                query_rows[0], key_rows[0], value_rows[0], gain_query[None], gain_key[None],
                out_weight, tokens[0], out_bias, gate_table,
            )
        )
    )
    return out[None]


def solution(mesh):
    placed = (
        P("frame", "seq", None), P("frame", "seq", None), P("frame", "seq", None), P("frame", "seq", None),
        P(), P(), P("seq", None), P(), P(), P(), P(),
    )
    return jax.shard_map(
        shards, mesh=mesh, in_specs=placed, out_specs=P("frame", "seq", None), check_vma=False
    )
```
